32 devices in a mesh: row: 4 (over y, core), col: 8 (over z, x).
Axes of the slice: x: 2, y: 2, z: 4, core: 2. Of those that a mesh axis runs over, the one named last changes fastest.
Arguments:
- elem_residual: bfloat16 [16384, 3, 256], P(('row', 'col')), may hold values from -6 to 6
- corners: int32 [16384, 3], P(('row', 'col')), may hold values from 0 to 383
- share_rows: int32 [32, 2, 64], P(('row', 'col')), may hold values from 0 to 255
- x_factor: bfloat16 [8192, 1728], P(('row', 'col')), may hold values from -0.40039062 to 0.40039062, as said below
Outputs:
- solution: float32 [8192, 256], P(('row', 'col'))
The draws below stay inside these ranges and needn't reach their ends.
Inputs may be any that keep to these rules, and one draw needn't show every extreme that they name: `corners`: values below 256 are own vertices, the next 64 the slots shared with the left neighbour, the last 64 those shared with the right neighbour. `share_rows`: own row indices; a row may appear several times. `x_factor`: independent entries, each column block with its own scale.
All inputs are finite; a program needn't handle non-finite values.
Results may differ from the reference program's by a relative error of at most 0.0035.
Values sent between devices are 32-bit elements; how exact they have to be, the bound alone decides.
A program may use at most 64 MiB of HBM per device.

```python
import jax
import jax.numpy as jnp
from jax import lax

RHS = 256
ROWS_DEV = 256
ELEMS = 512
SHARED = 64
INNER = 1408
SEP_COLS = 64
LEVELS = 5
COLS = 1728
ROWS = 8192
N_ROW = 4
N_COL = 8
DEVICES = 32


def draw_x_factor(key, part):
    columns = jnp.arange(COLS, dtype=jnp.int32)
    level = jnp.maximum(columns - INNER, 0) // SEP_COLS + 1
    level_scale = (jnp.exp2(level.astype(jnp.float32)) * ROWS_DEV * SEP_COLS) ** (-0.25)
    inner_scale = jnp.float32(ROWS_DEV * INNER) ** (-0.25)
    scales = jnp.where(columns < INNER, inner_scale, level_scale)
    entries = jnp.clip(jax.random.normal(jax.random.fold_in(key, 7), (ROWS, COLS), jnp.float32), -5.3, 5.3)
    return jnp.clip(entries * scales[None, :], -0.4, 0.4).astype(jnp.bfloat16)


def plant(array, stream_key, low, top_value):
    dims = array.shape
    index_at = [jax.random.randint(jax.random.fold_in(stream_key, axis), (), 0, dims[axis]) for axis in range(len(dims))]
    array = array.at[tuple(index_at)].set(low)
    longest = dims.index(max(dims))
    index_at[longest] = (index_at[longest] + 1) % dims[longest]
    return array.at[tuple(index_at)].set(top_value)


def block_levels(rng, shape, pieces, smallest, high):
    level, own = 1.0, jax.random.fold_in(rng, 6)
    for dim, parts in pieces:
        heights = jnp.exp(jax.random.uniform(jax.random.fold_in(own, dim), (parts,), jnp.float32, smallest / len(pieces), high / len(pieces)))
        level = level * jnp.repeat(heights, shape[dim] // parts).reshape([-1 if axis == dim else 1 for axis in range(len(shape))])
    return level


def centred(rng, shape, deviation, reach, pieces=(), kind=jnp.bfloat16):
    drawn = jax.random.normal(rng, shape, jnp.float32) * deviation
    if len(pieces) > 0:
        drawn = block_levels(rng, shape, pieces, -0.22, 0.18) * drawn
    return jnp.clip(drawn, min=-reach, max=reach).astype(kind)


def setup_inputs(seed: int = 0) -> dict:
    keys = jax.random.split(jax.random.key(seed), 5)
    return {
        "elem_residual": centred(keys[0], (DEVICES * ELEMS, 3, RHS), 1.0, 6.0, ((0, 32),)),
        "corners": plant(jax.random.randint(keys[1], (DEVICES * ELEMS, 3), 0, ROWS_DEV + 2 * SHARED), jax.random.fold_in(keys[1], 1), 0, (ROWS_DEV + 2 * SHARED) - 1).astype(jnp.int32),
        "share_rows": plant(jax.random.randint(keys[2], (DEVICES, 2, SHARED), 0, ROWS_DEV), jax.random.fold_in(keys[2], 1), 0, ROWS_DEV - 1).astype(jnp.int32),
        "x_factor": draw_x_factor(jax.random.fold_in(keys[4], 71), 0),
    }


def reference(elem_residual, corners, share_rows, x_factor):
    count = N_ROW * N_COL
    ext_len = ROWS_DEV + 2 * SHARED
    offsets = jnp.arange(count, dtype=jnp.int32)
    ids = corners.reshape(count, ELEMS * 3) + (offsets * ext_len)[:, None]
    values = elem_residual.astype(jnp.float32).reshape(count * ELEMS * 3, RHS)
    extended = jax.ops.segment_sum(values, ids.reshape(-1), num_segments=count * ext_len)
    extended = extended.reshape(N_ROW, N_COL, ext_len, RHS)
    owned = extended[:, :, :ROWS_DEV].reshape(count * ROWS_DEV, RHS)
    to_left = extended[:, :, ROWS_DEV:ROWS_DEV + SHARED]
    to_right = extended[:, :, ROWS_DEV + SHARED:]
    from_left = jnp.roll(to_right, 1, axis=1)
    from_right = jnp.roll(to_left, -1, axis=1)
    received = jnp.concatenate([from_left, from_right], axis=2).reshape(count * 2 * SHARED, RHS)
    targets = (share_rows.reshape(count, 2 * SHARED) + (offsets * ROWS_DEV)[:, None]).reshape(-1)
    assembled = owned + jax.ops.segment_sum(received, targets, num_segments=count * ROWS_DEV)
    rhs_local = assembled.astype(jnp.bfloat16).reshape(count, ROWS_DEV, RHS)
    factor = x_factor.reshape(count, ROWS_DEV, COLS)

    def inner_part(pair):
        block, local = pair
        inner = block[:, :INNER]
        weights = jnp.dot(inner.T, local, preferred_element_type=jnp.float32).astype(jnp.bfloat16)
        return jnp.dot(inner, weights, preferred_element_type=jnp.float32)

    solution = lax.map(inner_part, (factor, rhs_local))

    def separator_part(pair):
        block, local = pair
        return jnp.dot(block[:, INNER:].T, local, preferred_element_type=jnp.float32)

    partial_value = lax.map(separator_part, (factor, rhs_local)).reshape(count, LEVELS, SEP_COLS, RHS)
    summed = []
    for level in range(LEVELS):
        group = 2 ** (level + 1)
        totals = partial_value[:, level].reshape(count // group, group, SEP_COLS, RHS).sum(axis=1)
        summed.append(jnp.repeat(totals, group, axis=0).astype(jnp.bfloat16))
    coef = jnp.stack(summed, axis=1).reshape(count, LEVELS * SEP_COLS, RHS)

    def apply_part(pair):
        block, weights = pair
        return jnp.dot(block[:, INNER:], weights, preferred_element_type=jnp.float32)

    solution = solution + lax.map(apply_part, (factor, coef))
    return solution.reshape(count * ROWS_DEV, RHS)
```

```python
import functools

import jax
import jax.numpy as jnp
from jax import lax
from jax.experimental import pallas as pl
from jax.experimental.pallas import tpu as pltpu
from jax.sharding import PartitionSpec as P

INNER = 1408
MESH = pl.DeviceIdType.MESH
F32 = jnp.float32
BF16 = jnp.bfloat16


def swapped(block, axis, stride):
    count = lax.axis_size(axis)
    route = []
    for low in range(count):
        high = low | 1 << stride
        if high != low and high < count:
            route += [(low, high), (high, low)]
    return lax.ppermute(block, axis, route)


def summed_levels(blocks, n_row, n_col):
    col_bits = n_col.bit_length() - 1
    row_bits = n_row.bit_length() - 1
    for bit in range(col_bits + row_bits):
        axis, stride = ("col", bit) if bit < col_bits else ("row", bit - col_bits)
        partner = swapped(blocks[bit:], axis, stride)
        blocks = jnp.concatenate([blocks[:bit], blocks[bit:] + partner], axis=0)
    return blocks


def by_rounds(n_row, n_col, elem_residual, corners, share_rows, x_factor):
    rows_dev = x_factor.shape[0]
    shared = share_rows.shape[2]
    width = elem_residual.shape[2]
    levels = (n_row * n_col).bit_length() - 1
    ext_len = rows_dev + 2 * shared
    flat_ids = corners.reshape(-1)
    onehot = (
        lax.broadcasted_iota(jnp.int32, (ext_len, flat_ids.shape[0]), 0) == flat_ids[None, :]
    ).astype(BF16)
    extended = jnp.dot(onehot, elem_residual.reshape(-1, width), preferred_element_type=F32)
    forward = [(i, (i + 1) % n_col) for i in range(n_col)]
    backward = [(target, source) for source, target in forward]
    from_left = lax.ppermute(extended[rows_dev + shared :], "col", forward)
    from_right = lax.ppermute(extended[rows_dev : rows_dev + shared], "col", backward)
    row_ids = lax.broadcasted_iota(jnp.int32, (rows_dev, shared), 0)
    assembled = extended[:rows_dev]
    for side, received in ((0, from_left), (1, from_right)):
        side_map = (row_ids == share_rows[0, side][None, :]).astype(F32)
        assembled = assembled + jnp.dot(
            side_map, received, precision=lax.Precision.HIGHEST, preferred_element_type=F32
        )
    partial_value = lax.dot_general(
        x_factor, assembled.astype(BF16), (((0,), (0,)), ((), ())), preferred_element_type=F32
    )
    blocks = partial_value[INNER:].reshape(levels, -1, width)
    blocks = summed_levels(blocks, n_row, n_col)
    coef = jnp.concatenate([partial_value[:INNER], blocks.reshape(-1, width)], axis=0)
    return jnp.dot(x_factor, coef.astype(BF16), preferred_element_type=F32)


class Plan:
    def __init__(self, n_row, n_col, sep):
        self.n_row, self.n_col, self.sep = n_row, n_col, sep
        self.levels = (n_row * n_col).bit_length() - 1
        self.col_bits = n_col.bit_length() - 1
        self.wide = list(range(self.levels, self.col_bits - 1, -1))
        self.narrow = list(range(self.col_bits - 1, 1, -1))

    def row_span(self, level):
        return max(1, 2**level // self.n_col)

    def row_step(self, level):
        return self.n_col // 2 * self.row_span(level) // self.n_owners(level)

    def n_owners(self, level):
        return min(self.n_col // 2 * self.row_span(level), self.sep // 8)

    def piece(self, level):
        return self.sep // self.n_owners(level)

    def owners(self, level):
        rows = range(0, self.row_span(level), self.row_step(level))
        return [(r, self.n_col // 4 + c) for r in rows for c in range(self.n_col // 2)]

    def members(self, level):
        every = [(r, c) for r in range(self.row_span(level)) for c in range(self.n_col)]
        return sorted(every, key=lambda at: (at[1] // 2, at[0] % 2, at[1], at[0]))


def takes(n_row, n_col, sep):
    return n_col >= 4 and 2 <= n_row <= 4 and sep % (8 * n_col) == 0


def tdot(a, b):
    return lax.dot_general(a, b, (((0,), (0,)), ((), ())), preferred_element_type=F32)


def kernel(
    plan,
    er_hbm, cor_hbm, sh_hbm, x_hbm,
    out_ref,
    er, cor, sh, xt,
    halo_out, halo_in, own, rhs, part, l1_in, near_in, final, turned,
    in_sem, halo_s, halo_r, l1_s, l1_r, near_s, near_r, near_gs, near_gr, wide_s, wide_r, ag_s, ag_r,
    *wide_in,
):
    row, col = lax.axis_index("row"), lax.axis_index("col")
    levels, n_row, n_col, sep = plan.levels, plan.n_row, plan.n_col, plan.sep
    rows_dev = out_ref.shape[0]
    shared = halo_out.shape[1]
    kinds = er.shape[0]
    elems = er.shape[1]
    inner = xt.shape[0] - sep * levels
    wide_in = dict(zip(plan.wide, wide_in))

    right = (row, (col + 1) % n_col)
    left = (row, (col + n_col - 1) % n_col)
    first, last = n_col // 4, n_col // 4 * 3
    central = jnp.logical_and(col >= first, col < last)

    def col_peer(span, m):
        local = col % span
        return (row, col - local + (local + m) % span)

    def is_me(r, c):
        return jnp.logical_and(row == r, col == c)

    barrier = pltpu.get_barrier_semaphore()

    def greet(peer):
        pl.semaphore_signal(barrier, inc=1, device_id=peer, device_id_type=MESH)

    greet(left)
    greet(right)
    for level in plan.narrow:
        for m in range(1, 2**level):
            greet(col_peer(2**level, m))
    near = 2 + sum(2**level - 1 for level in plan.narrow)

    @pl.when(central)
    def _():
        for r in range(1, n_row):
            greet(((row + r) % n_row, col))
        for r in range(n_row):
            for c in range(1, n_col):
                greet(((row + r) % n_row, (col + c) % n_col))

    loads = [
        pltpu.make_async_copy(source, target, in_sem.at[i])
        for i, (source, target) in enumerate(
            ((cor_hbm, cor), (er_hbm, er), (sh_hbm, sh), (x_hbm, xt))
        )
    ]
    for load in loads:
        load.start()

    def assembled_rows(start, count):
        total = None
        for k in range(kinds):
            ids = cor[k : k + 1, :]
            at = lax.broadcasted_iota(jnp.int32, (count, elems), 0) + start
            onehot = jnp.where(at == ids, 1.0, 0.0).astype(BF16)
            term = jnp.dot(onehot, er[k], preferred_element_type=F32)
            total = term if total is None else total + term
        return total

    loads[0].wait()
    loads[1].wait()
    halo_out[...] = assembled_rows(rows_dev, 2 * shared).reshape(halo_out.shape)
    own[...] = assembled_rows(0, rows_dev)
    pl.semaphore_wait(barrier, near + n_row * n_col // 2 - central.astype(jnp.int32))

    def remote(source, target, send, recv, peer):
        return pltpu.make_async_remote_copy(
            src_ref=source,
            dst_ref=target,
            send_sem=send,
            recv_sem=recv,
            device_id=peer,
            device_id_type=MESH,
        )

    def sending(*args):
        copy = remote(*args)
        copy.start()
        return copy

    sent = []
    halo = [
        sending(halo_out.at[1], halo_in.at[0], halo_s.at[0], halo_r.at[0], right),
        sending(halo_out.at[0], halo_in.at[1], halo_s.at[1], halo_r.at[1], left),
    ]
    sent += halo

    loads[2].wait()
    targets = jnp.concatenate([sh[0:1, :], sh[1:2, :]], axis=1)
    at = lax.broadcasted_iota(jnp.int32, (rows_dev, 2 * shared), 0)
    share_map = jnp.where(at == targets, 1.0, 0.0).astype(BF16)
    share_map = jnp.concatenate([share_map, share_map], axis=1)
    loads[3].wait()
    turned[...] = xt[inner:, :].T
    for copy in halo:
        copy.wait_recv()
    received = halo_in[...].reshape(2 * shared, -1)
    high = received.astype(BF16)
    low = (received - high.astype(F32)).astype(BF16)
    received = jnp.concatenate([high, low], axis=0)
    assembled = own[...] + jnp.dot(share_map, received, preferred_element_type=F32)
    rhs[...] = assembled.astype(BF16)

    def partial(low, high):
        rows = xt[inner + sep * (low - 1) : inner + sep * high, :]
        block = jnp.dot(rows, rhs[...], preferred_element_type=F32)
        part[low - 1 : high] = block.reshape(high - low + 1, sep, -1)

    def place(level):
        span = plan.row_span(level)
        return row - row % span, row % span * n_col + col

    def owned(level):
        span, step = plan.row_span(level), plan.row_step(level)
        mine = jnp.logical_and(central, row % span % step == 0)
        index = row % span // step * (n_col // 2) + (col - first)
        rows = plan.piece(level)
        return mine, pl.ds(pl.multiple_of(jnp.where(mine, index, 0) * rows, 8), rows)

    def scatter(level):
        base, here = place(level)
        rows = plan.piece(level)
        for o, (r, c) in enumerate(plan.owners(level)):
            copy = remote(
                part.at[level - 1, pl.ds(o * rows, rows)],
                wide_in[level].at[here],
                wide_s.at[level - 1],
                wide_r.at[level - 1],
                (base + r, c),
            )

            @pl.when(jnp.logical_not(is_me(base + r, c)))
            def _():
                copy.start()

    def gather(level, some):
        base, _ = place(level)
        mine, rows = owned(level)
        block = final.at[level - 1, rows]

        @pl.when(mine)
        def _():
            for r, c in plan.members(level):
                if c in some:
                    copy = remote(block, block, ag_s.at[level - 1], ag_r.at[level - 1], (base + r, c))

                    @pl.when(jnp.logical_not(is_me(base + r, c)))
                    def _():
                        copy.start()

    def taken(buffer, sem):
        return pltpu.make_async_copy(buffer, buffer, sem)

    partial(plan.wide[-1], levels)
    for level in plan.wide:
        scatter(level)
    partial(1, plan.wide[-1] - 1)
    pair = sending(part.at[0], l1_in, l1_s.at[0], l1_r.at[0], col_peer(2, 1))
    sent.append(pair)

    def near_rows(level, ahead=0):
        span, rows = 2**level, sep // 2**level
        return pl.ds(pl.multiple_of((col % span + ahead) % span * rows, 8), rows)

    near_rs, near_ag = {}, {}
    for level in plan.narrow:
        for m in range(1, 2**level):
            near_rs[level, m] = sending(
                part.at[level - 1, near_rows(level, m)],
                near_in.at[level - 1, m - 1, pl.ds(0, sep // 2**level)],
                near_s.at[level - 1, m - 1],
                near_r.at[level - 1, m - 1],
                col_peer(2**level, m),
            )
    weights = jnp.dot(xt[:inner, :], rhs[...], preferred_element_type=F32).astype(BF16)
    out_ref[...] = tdot(xt[:inner, :], weights)

    early = range(2)
    for level in plan.wide:
        mine, rows = owned(level)
        _, here = place(level)
        count = wide_in[level].shape[0]

        @pl.when(mine)
        def _():
            wide_in[level][here] = part[level - 1, rows]
            taken(wide_in[level].at[pl.ds(0, count - 1)], wide_r.at[level - 1]).wait()
            total = wide_in[level][0]
            for k in range(1, count):
                total = total + wide_in[level][k]
            final[level - 1, rows] = total

        gather(level, early)
    for level in plan.narrow:
        rows = sep // 2**level
        total = part[level - 1, near_rows(level)]
        for m in range(1, 2**level):
            near_rs[level, m].wait_recv()
            total = total + near_in[level - 1, m - 1, pl.ds(0, rows)]
        final[level - 1, near_rows(level)] = total
        block = final.at[level - 1, near_rows(level)]
        for m in range(1, 2**level):
            near_ag[level, m] = sending(
                block, block, near_gs.at[level - 1, m - 1], near_gr.at[level - 1, m - 1], col_peer(2**level, m)
            )
    for level in plan.wide:
        gather(level, range(len(early), n_col))

    def applied(low, high):
        coef = final[low - 1 : high].reshape(sep * (high - low + 1), -1).astype(BF16)
        return jnp.dot(turned[:, sep * (low - 1) : sep * high], coef, preferred_element_type=F32)

    pair.wait_recv()
    final[0] = part[0] + l1_in[...]
    for copy in near_ag.values():
        copy.wait_recv()
    low = plan.wide[-1] - 1
    out_ref[...] += applied(1, low)

    for level in plan.wide:
        mine, _ = owned(level)
        others = sep - plan.piece(level)

        @pl.when(mine)
        def _():
            taken(final.at[level - 1, pl.ds(0, others)], ag_r.at[level - 1]).wait()

        @pl.when(jnp.logical_not(mine))
        def _():
            taken(final.at[level - 1], ag_r.at[level - 1]).wait()

    out_ref[...] += applied(low + 1, levels)
    sent += list(near_rs.values()) + list(near_ag.values())
    for copy in sent:
        copy.wait_send()
    for level in plan.wide:
        mine, _ = owned(level)
        others = sep - plan.piece(level)
        count = wide_in[level].shape[0]

        @pl.when(mine)
        def _():
            taken(part.at[level - 1, pl.ds(0, others)], wide_s.at[level - 1]).wait()
            taken(wide_in[level].at[pl.ds(0, count - 1)], ag_s.at[level - 1]).wait()

        @pl.when(jnp.logical_not(mine))
        def _():
            taken(part.at[level - 1], wide_s.at[level - 1]).wait()


def in_one_kernel(plan, elem_residual, corners, share_rows, x_factor):
    rows_dev, cols = x_factor.shape
    shared = share_rows.shape[2]
    elems, kinds, width = elem_residual.shape
    levels, sep = plan.levels, plan.sep
    slots = max(1, plan.n_col // 2 - 1)
    dma = pltpu.SemaphoreType.DMA
    anywhere = pl.BlockSpec(memory_space=pl.ANY)
    return pl.pallas_call(
        functools.partial(kernel, plan),
        out_shape=pltpu.VMEM((rows_dev, width), F32),
        in_specs=[anywhere] * 4,
        out_specs=pl.BlockSpec(memory_space=pltpu.VMEM),
        scratch_shapes=[
            pltpu.VMEM((kinds, elems, width), BF16),
            pltpu.VMEM((kinds, elems), jnp.int32),
            pltpu.VMEM((2, shared), jnp.int32),
            pltpu.VMEM((cols, rows_dev), BF16),
            pltpu.VMEM((2, shared, width), F32),
            pltpu.VMEM((2, shared, width), F32),
            pltpu.VMEM((rows_dev, width), F32),
            pltpu.VMEM((rows_dev, width), BF16),
            pltpu.VMEM((levels, sep, width), F32),
            pltpu.VMEM((sep, width), F32),
            pltpu.VMEM((levels, slots, sep // 4, width), F32),
            pltpu.VMEM((levels, sep, width), F32),
            pltpu.VMEM((rows_dev, sep * levels), BF16),
            dma((4,)),
            dma((2,)),
            dma((2,)),
            dma((1,)),
            dma((1,)),
            dma((levels, slots)),
            dma((levels, slots)),
            dma((levels, slots)),
            dma((levels, slots)),
            dma((levels,)),
            dma((levels,)),
            dma((levels,)),
            dma((levels,)),
        ]
        + [
            pltpu.VMEM((plan.row_span(level) * plan.n_col, plan.piece(level), width), F32)
            for level in plan.wide
        ],
        compiler_params=pltpu.CompilerParams(collective_id=0, has_side_effects=True),
        name="factor_solve",
    )(
        elem_residual.transpose(1, 0, 2),
        corners.T,
        share_rows.reshape(2, shared),
        x_factor.T,
    )


def solution(mesh):
    n_row, n_col = mesh.shape["row"], mesh.shape["col"]
    levels = (n_row * n_col).bit_length() - 1

    def per_device(elem_residual, corners, share_rows, x_factor):
        sep = (x_factor.shape[1] - INNER) // levels
        args = (elem_residual, corners, share_rows, x_factor)
        if takes(n_row, n_col, sep):
            return in_one_kernel(Plan(n_row, n_col, sep), *args)
        return by_rounds(n_row, n_col, *args)

    placed = (
        P(("row", "col"), None, None),
        P(("row", "col"), None),
        P(("row", "col"), None, None),
        P(("row", "col"), None),
    )
    return jax.shard_map(
        per_device, mesh=mesh, in_specs=placed, out_specs=P(("row", "col"), None), check_vma=False
    )
```

```python
import functools

import jax
import jax.numpy as jnp
from jax import lax
from jax.experimental import pallas as pl
from jax.experimental.pallas import tpu as pltpu
from jax.sharding import PartitionSpec as P

INNER = 1408
MESH = pl.DeviceIdType.MESH
F32 = jnp.float32
BF16 = jnp.bfloat16


def swapped(block, axis, stride):
    count = lax.axis_size(axis)
    route = []
    for low in range(count):
        high = low | 1 << stride
        if high != low and high < count:
            route += [(low, high), (high, low)]
    return lax.ppermute(block, axis, route)


def summed_levels(blocks, n_row, n_col):
    col_bits = n_col.bit_length() - 1
    row_bits = n_row.bit_length() - 1
    for bit in range(col_bits + row_bits):
        axis, stride = ("col", bit) if bit < col_bits else ("row", bit - col_bits)
        partner = swapped(blocks[bit:], axis, stride)
        blocks = jnp.concatenate([blocks[:bit], blocks[bit:] + partner], axis=0)
    return blocks


def by_rounds(n_row, n_col, elem_residual, corners, share_rows, x_factor):
    rows_dev = x_factor.shape[0]
    shared = share_rows.shape[2]
    width = elem_residual.shape[2]
    levels = (n_row * n_col).bit_length() - 1
    ext_len = rows_dev + 2 * shared
    flat_ids = corners.reshape(-1)
    onehot = (
        lax.broadcasted_iota(jnp.int32, (ext_len, flat_ids.shape[0]), 0) == flat_ids[None, :]
    ).astype(BF16)
    extended = jnp.dot(onehot, elem_residual.reshape(-1, width), preferred_element_type=F32)
    forward = [(i, (i + 1) % n_col) for i in range(n_col)]
    backward = [(target, source) for source, target in forward]
    from_left = lax.ppermute(extended[rows_dev + shared :], "col", forward)
    from_right = lax.ppermute(extended[rows_dev : rows_dev + shared], "col", backward)
    row_ids = lax.broadcasted_iota(jnp.int32, (rows_dev, shared), 0)
    assembled = extended[:rows_dev]
    for side, received in ((0, from_left), (1, from_right)):
        side_map = (row_ids == share_rows[0, side][None, :]).astype(F32)
        assembled = assembled + jnp.dot(
            side_map, received, precision=lax.Precision.HIGHEST, preferred_element_type=F32
        )
    partial_value = lax.dot_general(
        x_factor, assembled.astype(BF16), (((0,), (0,)), ((), ())), preferred_element_type=F32
    )
    blocks = partial_value[INNER:].reshape(levels, -1, width)
    blocks = summed_levels(blocks, n_row, n_col)
    coef = jnp.concatenate([partial_value[:INNER], blocks.reshape(-1, width)], axis=0)
    return jnp.dot(x_factor, coef.astype(BF16), preferred_element_type=F32)


class Plan:
    def __init__(self, n_row, n_col, sep):
        self.n_row, self.n_col, self.sep = n_row, n_col, sep
        self.levels = (n_row * n_col).bit_length() - 1
        self.col_bits = n_col.bit_length() - 1
        self.wide = list(range(self.col_bits, self.levels + 1))
        self.upper = self.wide[1:]
        self.narrow = list(range(self.col_bits - 1, 1, -1))

    def row_span(self, level):
        return max(1, 2**level // self.n_col)

    def halves(self, level):
        return 2 if self.row_span(level) > 1 else 1

    def piece(self, level):
        return self.sep // (self.n_col // 2 * self.halves(level))

    def sources(self, level):
        return self.row_span(level) // self.halves(level) * self.n_col

    def members(self, level):
        every = [(r, c) for r in range(self.row_span(level)) for c in range(self.n_col)]
        return sorted(every, key=lambda at: (at[1] // 2, at[0] % 2, at[1], at[0]))


def takes(n_row, n_col, sep):
    return n_col >= 4 and 2 <= n_row <= 4 and sep % (8 * n_col) == 0


def tdot(a, b):
    return lax.dot_general(a, b, (((0,), (0,)), ((), ())), preferred_element_type=F32)


def kernel(
    plan,
    er_hbm, cor_hbm, sh_hbm, x_hbm,
    out_ref,
    er, cor, sh, xt,
    halo_out, halo_in, own, rhs, part, l1_in, pair_in, near_in, final, turned,
    in_sem, halo_s, halo_r, pair_s, pair_r, l1_s, l1_r, near_s, near_r, near_gs, near_gr, wide_s, wide_r, ag_s, ag_r,
    *wide_in,
):
    row, col = lax.axis_index("row"), lax.axis_index("col")
    levels, n_row, n_col, sep = plan.levels, plan.n_row, plan.n_col, plan.sep
    rows_dev = out_ref.shape[0]
    shared = halo_out.shape[1]
    kinds = er.shape[0]
    elems = er.shape[1]
    inner = xt.shape[0] - sep * levels
    wide_in = dict(zip(plan.wide, wide_in))

    right = (row, (col + 1) % n_col)
    left = (row, (col + n_col - 1) % n_col)
    first, last = n_col // 4, n_col // 4 * 3
    central = jnp.logical_and(col >= first, col < last)

    def col_peer(span, m):
        local = col % span
        return (row, col - local + (local + m) % span)

    def is_me(r, c):
        return jnp.logical_and(row == r, col == c)

    barrier = pltpu.get_barrier_semaphore()

    def greet(peer):
        pl.semaphore_signal(barrier, inc=1, device_id=peer, device_id_type=MESH)

    greet(left)
    greet(right)
    greet((row ^ 1, col))
    for level in plan.narrow:
        for m in range(1, 2**level):
            greet(col_peer(2**level, m))
    near = 3 + sum(2**level - 1 for level in plan.narrow)

    @pl.when(central)
    def _():
        for r in range(1, n_row):
            greet(((row + r) % n_row, col))
        for r in range(n_row):
            for c in range(1, n_col):
                greet(((row + r) % n_row, (col + c) % n_col))

    loads = [
        pltpu.make_async_copy(source, target, in_sem.at[i])
        for i, (source, target) in enumerate(
            ((cor_hbm, cor), (er_hbm, er), (sh_hbm, sh), (x_hbm, xt))
        )
    ]
    for load in loads:
        load.start()

    def assembled_rows(start, count):
        total = None
        for k in range(kinds):
            ids = cor[k : k + 1, :]
            at = lax.broadcasted_iota(jnp.int32, (count, elems), 0) + start
            onehot = jnp.where(at == ids, 1.0, 0.0).astype(BF16)
            term = jnp.dot(onehot, er[k], preferred_element_type=F32)
            total = term if total is None else total + term
        return total

    loads[0].wait()
    loads[1].wait()
    halo_out[...] = assembled_rows(rows_dev, 2 * shared).reshape(halo_out.shape)
    own[...] = assembled_rows(0, rows_dev)
    pl.semaphore_wait(barrier, near + n_row * n_col // 2 - central.astype(jnp.int32))

    def remote(source, target, send, recv, peer):
        return pltpu.make_async_remote_copy(
            src_ref=source,
            dst_ref=target,
            send_sem=send,
            recv_sem=recv,
            device_id=peer,
            device_id_type=MESH,
        )

    def sending(*args):
        copy = remote(*args)
        copy.start()
        return copy

    sent = []
    halo = [
        sending(halo_out.at[1], halo_in.at[0], halo_s.at[0], halo_r.at[0], right),
        sending(halo_out.at[0], halo_in.at[1], halo_s.at[1], halo_r.at[1], left),
    ]
    sent += halo

    loads[2].wait()
    targets = jnp.concatenate([sh[0:1, :], sh[1:2, :]], axis=1)
    at = lax.broadcasted_iota(jnp.int32, (rows_dev, 2 * shared), 0)
    share_map = jnp.where(at == targets, 1.0, 0.0).astype(BF16)
    share_map = jnp.concatenate([share_map, share_map], axis=1)
    loads[3].wait()
    turned[...] = xt[inner:, :].T
    for copy in halo:
        copy.wait_recv()
    received = halo_in[...].reshape(2 * shared, -1)
    high = received.astype(BF16)
    low = (received - high.astype(F32)).astype(BF16)
    received = jnp.concatenate([high, low], axis=0)
    assembled = own[...] + jnp.dot(share_map, received, preferred_element_type=F32)
    rhs[...] = assembled.astype(BF16)

    def partial(low, high):
        rows = xt[inner + sep * (low - 1) : inner + sep * high, :]
        block = jnp.dot(rows, rhs[...], preferred_element_type=F32)
        part[low - 1 : high] = block.reshape(high - low + 1, sep, -1)

    half = row % 2

    def owned(level):
        span, halves = plan.row_span(level), plan.halves(level)
        base = row - row % span
        mine = jnp.logical_and(central, row == base + half * (span - 1))
        index = half * (halves - 1) * (n_col // 2) + (col - first)
        rows = plan.piece(level)
        slot = row % span // halves * n_col + col
        return mine, pl.ds(pl.multiple_of(jnp.where(mine, index, 0) * rows, 8), rows), slot, base

    def scatter(level):
        _, _, slot, base = owned(level)
        rows, halves = plan.piece(level), plan.halves(level)
        start = half * (halves - 1) * (sep // 2)
        target = base + half * (plan.row_span(level) - 1)
        for c in range(n_col // 2):
            copy = remote(
                part.at[level - 1, pl.ds(pl.multiple_of(start + c * rows, 8), rows)],
                wide_in[level].at[slot],
                wide_s.at[level - 1],
                wide_r.at[level - 1],
                (target, first + c),
            )

            @pl.when(jnp.logical_not(is_me(target, first + c)))
            def _():
                copy.start()

    def gather(level, some):
        mine, rows, _, base = owned(level)
        block = final.at[level - 1, rows]

        @pl.when(mine)
        def _():
            for r, c in plan.members(level):
                if c in some:
                    copy = remote(block, block, ag_s.at[level - 1], ag_r.at[level - 1], (base + r, c))

                    @pl.when(jnp.logical_not(is_me(base + r, c)))
                    def _():
                        copy.start()

    def taken(buffer, sem):
        return pltpu.make_async_copy(buffer, buffer, sem)

    partial(plan.wide[0], levels)
    kept = pl.ds(pl.multiple_of(half * (sep // 2), 8), sep // 2)
    given = pl.ds(pl.multiple_of((1 - half) * (sep // 2), 8), sep // 2)
    over = pl.ds(plan.upper[0] - 1, len(plan.upper))
    cores = sending(part.at[over, given], pair_in, pair_s.at[0], pair_r.at[0], (row ^ 1, col))
    sent.append(cores)
    scatter(plan.wide[0])
    cores.wait_recv()
    for i, level in enumerate(plan.upper):
        part[level - 1, kept] += pair_in[i]
    for level in reversed(plan.upper):
        scatter(level)
    partial(1, plan.wide[0] - 1)
    pair = sending(part.at[0], l1_in, l1_s.at[0], l1_r.at[0], col_peer(2, 1))
    sent.append(pair)

    def near_rows(level, ahead=0):
        span, rows = 2**level, sep // 2**level
        return pl.ds(pl.multiple_of((col % span + ahead) % span * rows, 8), rows)

    near_rs, near_ag = {}, {}
    for level in plan.narrow:
        for m in range(1, 2**level):
            near_rs[level, m] = sending(
                part.at[level - 1, near_rows(level, m)],
                near_in.at[level - 1, m - 1, pl.ds(0, sep // 2**level)],
                near_s.at[level - 1, m - 1],
                near_r.at[level - 1, m - 1],
                col_peer(2**level, m),
            )
    weights = jnp.dot(xt[:inner, :], rhs[...], preferred_element_type=F32).astype(BF16)
    out_ref[...] = tdot(xt[:inner, :], weights)

    early = range(2)
    for level in plan.wide[:1] + plan.upper[::-1]:
        mine, rows, slot, _ = owned(level)
        count = plan.sources(level)

        @pl.when(mine)
        def _():
            wide_in[level][slot] = part[level - 1, rows]
            taken(wide_in[level].at[pl.ds(0, count - 1)], wide_r.at[level - 1]).wait()
            total = wide_in[level][0]
            for k in range(1, count):
                total = total + wide_in[level][k]
            final[level - 1, rows] = total

        gather(level, early)
    for level in plan.narrow:
        rows = sep // 2**level
        total = part[level - 1, near_rows(level)]
        for m in range(1, 2**level):
            near_rs[level, m].wait_recv()
            total = total + near_in[level - 1, m - 1, pl.ds(0, rows)]
        final[level - 1, near_rows(level)] = total
        block = final.at[level - 1, near_rows(level)]
        for m in range(1, 2**level):
            near_ag[level, m] = sending(
                block, block, near_gs.at[level - 1, m - 1], near_gr.at[level - 1, m - 1], col_peer(2**level, m)
            )
    for level in plan.wide:
        gather(level, range(len(early), n_col))

    def applied(low, high):
        coef = final[low - 1 : high].reshape(sep * (high - low + 1), -1).astype(BF16)
        return jnp.dot(turned[:, sep * (low - 1) : sep * high], coef, preferred_element_type=F32)

    pair.wait_recv()
    final[0] = part[0] + l1_in[...]
    for copy in near_ag.values():
        copy.wait_recv()
    low = plan.wide[0] - 1
    out_ref[...] += applied(1, low)

    for level in plan.wide:
        mine = owned(level)[0]
        others = sep - plan.piece(level)

        @pl.when(mine)
        def _():
            taken(final.at[level - 1, pl.ds(0, others)], ag_r.at[level - 1]).wait()

        @pl.when(jnp.logical_not(mine))
        def _():
            taken(final.at[level - 1], ag_r.at[level - 1]).wait()

    out_ref[...] += applied(low + 1, levels)
    sent += list(near_rs.values()) + list(near_ag.values())
    for copy in sent:
        copy.wait_send()
    for level in plan.wide:
        mine = owned(level)[0]
        mass = sep // plan.halves(level)
        rows = plan.piece(level)
        members = plan.row_span(level) * n_col

        @pl.when(mine)
        def _():
            taken(part.at[level - 1, pl.ds(0, mass - rows)], wide_s.at[level - 1]).wait()
            taken(wide_in[level].at[pl.ds(0, members - 1)], ag_s.at[level - 1]).wait()

        @pl.when(jnp.logical_not(mine))
        def _():
            taken(part.at[level - 1, pl.ds(0, mass)], wide_s.at[level - 1]).wait()


def in_one_kernel(plan, elem_residual, corners, share_rows, x_factor):
    rows_dev, cols = x_factor.shape
    shared = share_rows.shape[2]
    elems, kinds, width = elem_residual.shape
    levels, sep = plan.levels, plan.sep
    slots = max(1, plan.n_col // 2 - 1)
    dma = pltpu.SemaphoreType.DMA
    anywhere = pl.BlockSpec(memory_space=pl.ANY)
    return pl.pallas_call(
        functools.partial(kernel, plan),
        out_shape=pltpu.VMEM((rows_dev, width), F32),
        in_specs=[anywhere] * 4,
        out_specs=pl.BlockSpec(memory_space=pltpu.VMEM),
        scratch_shapes=[
            pltpu.VMEM((kinds, elems, width), BF16),
            pltpu.VMEM((kinds, elems), jnp.int32),
            pltpu.VMEM((2, shared), jnp.int32),
            pltpu.VMEM((cols, rows_dev), BF16),
            pltpu.VMEM((2, shared, width), F32),
            pltpu.VMEM((2, shared, width), F32),
            pltpu.VMEM((rows_dev, width), F32),
            pltpu.VMEM((rows_dev, width), BF16),
            pltpu.VMEM((levels, sep, width), F32),
            pltpu.VMEM((sep, width), F32),
            pltpu.VMEM((len(plan.upper), sep // 2, width), F32),
            pltpu.VMEM((levels, slots, sep // 4, width), F32),
            pltpu.VMEM((levels, sep, width), F32),
            pltpu.VMEM((rows_dev, sep * levels), BF16),
            dma((4,)),
            dma((2,)),
            dma((2,)),
            dma((1,)),
            dma((1,)),
            dma((1,)),
            dma((1,)),
            dma((levels, slots)),
            dma((levels, slots)),
            dma((levels, slots)),
            dma((levels, slots)),
            dma((levels,)),
            dma((levels,)),
            dma((levels,)),
            dma((levels,)),
        ]
        + [
            pltpu.VMEM((plan.row_span(level) * plan.n_col, plan.piece(level), width), F32)
            for level in plan.wide
        ],
        compiler_params=pltpu.CompilerParams(collective_id=0, has_side_effects=True),
        name="factor_solve",
    )(
        elem_residual.transpose(1, 0, 2),
        corners.T,
        share_rows.reshape(2, shared),
        x_factor.T,
    )


def solution(mesh):
    n_row, n_col = mesh.shape["row"], mesh.shape["col"]
    levels = (n_row * n_col).bit_length() - 1

    def per_device(elem_residual, corners, share_rows, x_factor):
        sep = (x_factor.shape[1] - INNER) // levels
        args = (elem_residual, corners, share_rows, x_factor)
        if takes(n_row, n_col, sep):
            return in_one_kernel(Plan(n_row, n_col, sep), *args)
        return by_rounds(n_row, n_col, *args)

    placed = (
        P(("row", "col"), None, None),
        P(("row", "col"), None),
        P(("row", "col"), None, None),
        P(("row", "col"), None),
    )
    return jax.shard_map(
        per_device, mesh=mesh, in_specs=placed, out_specs=P(("row", "col"), None), check_vma=False
    )
```

```python
import functools

import jax
import jax.numpy as jnp
from jax import lax
from jax.experimental import pallas as pl
from jax.experimental.pallas import tpu as pltpu
from jax.sharding import PartitionSpec as P

INNER = 1408
OUTER = (0, 2, 3, 1)
MESH = pl.DeviceIdType.MESH
F32 = jnp.float32
BF16 = jnp.bfloat16


def swapped(block, axis, stride):
    count = lax.axis_size(axis)
    route = []
    for low in range(count):
        high = low | 1 << stride
        if high != low and high < count:
            route += [(low, high), (high, low)]
    return lax.ppermute(block, axis, route)


def summed_levels(blocks, n_row, n_col):
    col_bits = n_col.bit_length() - 1
    row_bits = n_row.bit_length() - 1
    for bit in range(col_bits + row_bits):
        axis, stride = ("col", bit) if bit < col_bits else ("row", bit - col_bits)
        partner = swapped(blocks[bit:], axis, stride)
        blocks = jnp.concatenate([blocks[:bit], blocks[bit:] + partner], axis=0)
    return blocks


def by_rounds(n_row, n_col, elem_residual, corners, share_rows, x_factor):
    rows_dev = x_factor.shape[0]
    shared = share_rows.shape[2]
    width = elem_residual.shape[2]
    levels = (n_row * n_col).bit_length() - 1
    ext_len = rows_dev + 2 * shared
    flat_ids = corners.reshape(-1)
    onehot = (
        lax.broadcasted_iota(jnp.int32, (ext_len, flat_ids.shape[0]), 0) == flat_ids[None, :]
    ).astype(BF16)
    extended = jnp.dot(onehot, elem_residual.reshape(-1, width), preferred_element_type=F32)
    forward = [(i, (i + 1) % n_col) for i in range(n_col)]
    backward = [(target, source) for source, target in forward]
    from_left = lax.ppermute(extended[rows_dev + shared :], "col", forward)
    from_right = lax.ppermute(extended[rows_dev : rows_dev + shared], "col", backward)
    row_ids = lax.broadcasted_iota(jnp.int32, (rows_dev, shared), 0)
    assembled = extended[:rows_dev]
    for side, received in ((0, from_left), (1, from_right)):
        side_map = (row_ids == share_rows[0, side][None, :]).astype(F32)
        assembled = assembled + jnp.dot(
            side_map, received, precision=lax.Precision.HIGHEST, preferred_element_type=F32
        )
    partial_value = lax.dot_general(
        x_factor, assembled.astype(BF16), (((0,), (0,)), ((), ())), preferred_element_type=F32
    )
    blocks = partial_value[INNER:].reshape(levels, -1, width)
    blocks = summed_levels(blocks, n_row, n_col)
    coef = jnp.concatenate([partial_value[:INNER], blocks.reshape(-1, width)], axis=0)
    return jnp.dot(x_factor, coef.astype(BF16), preferred_element_type=F32)


class Plan:
    def __init__(self, n_row, n_col, sep):
        self.n_row, self.n_col, self.sep = n_row, n_col, sep
        self.levels = (n_row * n_col).bit_length() - 1
        self.col_bits = n_col.bit_length() - 1
        self.wide = list(range(self.col_bits, self.levels + 1))
        self.upper = self.wide[1:]
        self.narrow = list(range(self.col_bits - 1, 1, -1))

    def row_span(self, level):
        return max(1, 2**level // self.n_col)

    def halves(self, level):
        return 2 if self.row_span(level) > 1 else 1

    def piece(self, level):
        return self.sep // (self.n_col // 2 * self.halves(level))

    def sources(self, level):
        return self.row_span(level) // self.halves(level) * self.n_col

    def members(self, level):
        every = [(r, c) for r in range(self.row_span(level)) for c in range(self.n_col)]
        every = [at for at in every if at[0] % self.halves(level) == 0]
        return sorted(every, key=lambda at: (OUTER[at[1] * 4 // self.n_col], at[0] % 2, at[1], at[0]))


def takes(n_row, n_col, sep):
    return n_col >= 4 and 2 <= n_row <= 4 and sep % (8 * n_col) == 0


def tdot(a, b):
    return lax.dot_general(a, b, (((0,), (0,)), ((), ())), preferred_element_type=F32)


def kernel(
    plan,
    er_hbm, cor_hbm, sh_hbm, x_hbm,
    out_ref,
    er, cor, sh, xt,
    halo_out, halo_in, own, rhs, part, l1_in, pair_in, near_in, final, turned, shared_rows, passed_in,
    in_sem, halo_s, halo_r, pair_s, pair_r, passed_s, passed_r, l1_s, l1_r, near_s, near_r, near_gs, near_gr, wide_s, wide_r, ag_s, ag_r,
    *wide_in,
):
    row, col = lax.axis_index("row"), lax.axis_index("col")
    levels, n_row, n_col, sep = plan.levels, plan.n_row, plan.n_col, plan.sep
    rows_dev = out_ref.shape[0]
    shared = halo_out.shape[1]
    kinds = er.shape[0]
    elems = er.shape[1]
    wide_in = dict(zip(plan.wide, wide_in))

    right = (row, (col + 1) % n_col)
    left = (row, (col + n_col - 1) % n_col)
    first, last = n_col // 4, n_col // 4 * 3
    central = jnp.logical_and(col >= first, col < last)

    def col_peer(span, m):
        local = col % span
        return (row, col - local + (local + m) % span)

    def is_me(r, c):
        return jnp.logical_and(row == r, col == c)

    barrier = pltpu.get_barrier_semaphore()

    def greet(peer):
        pl.semaphore_signal(barrier, inc=1, device_id=peer, device_id_type=MESH)

    greet(left)
    greet(right)
    greet((row ^ 1, col))
    for level in plan.narrow:
        for m in range(1, 2**level):
            greet(col_peer(2**level, m))
    near = 3 + sum(2**level - 1 for level in plan.narrow)

    @pl.when(central)
    def _():
        for r in range(1, n_row):
            greet(((row + r) % n_row, col))
        for r in range(n_row):
            for c in range(1, n_col):
                greet(((row + r) % n_row, (col + c) % n_col))

    inner = xt.shape[0] - sep * levels
    low = plan.wide[0] - 1
    wide_at = inner + sep * low
    parts = [(cor_hbm, cor)]
    parts += [(er_hbm.at[k], er.at[k]) for k in range(kinds)]
    parts += [(sh_hbm, sh), (x_hbm.at[wide_at:], xt.at[wide_at:]), (x_hbm.at[:wide_at], xt.at[:wide_at])]
    loads = [
        pltpu.make_async_copy(source, target, in_sem.at[i]) for i, (source, target) in enumerate(parts)
    ]
    for load in loads[: kinds + 1]:
        load.start()

    def assembled_rows(start, count, start_done=True):
        total = None
        for k in range(kinds):
            if not start_done:
                loads[k + 1].wait()
            ids = cor[k : k + 1, :]
            at = lax.broadcasted_iota(jnp.int32, (count, elems), 0) + start
            onehot = jnp.where(at == ids, 1.0, 0.0).astype(BF16)
            term = jnp.dot(onehot, er[k], preferred_element_type=F32)
            total = term if total is None else total + term
        return total

    loads[0].wait()
    halo_out[...] = assembled_rows(rows_dev, 2 * shared, False).reshape(halo_out.shape)
    for load in loads[kinds + 1 :]:
        load.start()
    pl.semaphore_wait(barrier, near + n_row * n_col // 2 - central.astype(jnp.int32))

    def taken(buffer, sem):
        return pltpu.make_async_copy(buffer, buffer, sem)

    def remote(source, target, send, recv, peer):
        return pltpu.make_async_remote_copy(
            src_ref=source,
            dst_ref=target,
            send_sem=send,
            recv_sem=recv,
            device_id=peer,
            device_id_type=MESH,
        )

    def sending(*args):
        copy = remote(*args)
        copy.start()
        return copy

    sent = []
    away = col % 2
    near_side = 1 - away
    far_peer = (row, (col + n_col - 1 + 2 * away) % n_col)
    near_peer = (row, (col + n_col - 1 + 2 * near_side) % n_col)
    halo = [
        sending(halo_out.at[away], halo_in.at[near_side], halo_s.at[0], halo_r.at[near_side], far_peer),
        sending(halo_out.at[near_side], halo_in.at[away], halo_s.at[1], halo_r.at[away], near_peer),
    ]
    sent += halo

    def split(value):
        high = value.astype(BF16)
        return high, (value - high.astype(F32)).astype(BF16)

    own[...] = assembled_rows(0, rows_dev)
    loads[kinds + 1].wait()
    targets = jnp.concatenate([sh[0:1, :], sh[1:2, :]], axis=1)
    at = lax.broadcasted_iota(jnp.int32, (rows_dev, 2 * shared), 0)
    share_map = jnp.where(at == targets, 1.0, 0.0).astype(BF16)
    share_map = jnp.concatenate([share_map, share_map], axis=1)
    loads[kinds + 2].wait()
    rows = xt[wide_at:, :]
    high, fine = split(own[...])
    of_own = jnp.dot(rows, high, preferred_element_type=F32) + jnp.dot(rows, fine, preferred_element_type=F32)
    part[low:] = of_own.reshape(len(plan.wide), sep, -1)
    shared_rows[...] = jnp.dot(rows, share_map, preferred_element_type=F32).astype(BF16)
    loads[kinds + 3].wait()
    turned[...] = xt[inner:, :].T
    for side in range(2):
        taken(halo_in.at[side], halo_r.at[side]).wait()
    received = jnp.concatenate(split(halo_in[...].reshape(2 * shared, -1)), axis=0)
    block = jnp.dot(shared_rows[...], received, preferred_element_type=F32)
    part[low:] += block.reshape(len(plan.wide), sep, -1)

    half = row % 2

    def owned(level):
        span, halves = plan.row_span(level), plan.halves(level)
        base = row - row % span
        mine = jnp.logical_and(central, row == base + half * (span - 1))
        index = half * (halves - 1) * (n_col // 2) + (col - first)
        rows = plan.piece(level)
        slot = row % span // halves * n_col + col
        return mine, pl.ds(pl.multiple_of(jnp.where(mine, index, 0) * rows, 8), rows), slot, base

    def scatter(level):
        _, _, slot, base = owned(level)
        rows, halves = plan.piece(level), plan.halves(level)
        start = half * (halves - 1) * (sep // 2)
        target = base + half * (plan.row_span(level) - 1)
        for c in range(n_col // 2):
            copy = remote(
                part.at[level - 1, pl.ds(pl.multiple_of(start + c * rows, 8), rows)],
                wide_in[level].at[slot],
                wide_s.at[level - 1],
                wide_r.at[level - 1],
                (target, first + c),
            )

            @pl.when(jnp.logical_not(is_me(target, first + c)))
            def _():
                copy.start()

    def gather(level, some):
        mine, rows, _, base = owned(level)
        block = final.at[level - 1, rows]

        @pl.when(mine)
        def _():
            for r, c in plan.members(level):
                if c in some:
                    copy = remote(block, block, ag_s.at[level - 1], ag_r.at[level - 1], (base + r, c))

                    @pl.when(jnp.logical_not(is_me(base + r, c)))
                    def _():
                        copy.start()

    kept = pl.ds(pl.multiple_of(half * (sep // 2), 8), sep // 2)
    given = pl.ds(pl.multiple_of((1 - half) * (sep // 2), 8), sep // 2)
    over = pl.ds(plan.upper[0] - 1, len(plan.upper))
    cores = sending(part.at[over, given], pair_in, pair_s.at[0], pair_r.at[0], (row ^ 1, col))
    sent.append(cores)
    scatter(plan.wide[0])
    cores.wait_recv()
    for i, level in enumerate(plan.upper):
        part[level - 1, kept] += pair_in[i]
    for level in reversed(plan.upper):
        scatter(level)
    assembled = own[...] + jnp.dot(share_map, received, preferred_element_type=F32)
    rhs[...] = assembled.astype(BF16)
    block = jnp.dot(xt[inner:wide_at, :], rhs[...], preferred_element_type=F32)
    part[:low] = block.reshape(low, sep, -1)
    pair = sending(part.at[0], l1_in, l1_s.at[0], l1_r.at[0], col_peer(2, 1))
    sent.append(pair)

    def near_rows(level, ahead=0):
        span, rows = 2**level, sep // 2**level
        return pl.ds(pl.multiple_of((col % span + ahead) % span * rows, 8), rows)

    near_rs, near_ag = {}, {}
    for level in plan.narrow:
        for m in range(1, 2**level):
            near_rs[level, m] = sending(
                part.at[level - 1, near_rows(level, m)],
                near_in.at[level - 1, m - 1, pl.ds(0, sep // 2**level)],
                near_s.at[level - 1, m - 1],
                near_r.at[level - 1, m - 1],
                col_peer(2**level, m),
            )
    weights = jnp.dot(xt[:inner, :], rhs[...], preferred_element_type=F32).astype(BF16)
    out_ref[...] = tdot(xt[:inner, :], weights)

    outer = [c for c in range(n_col) if OUTER[c * 4 // n_col] < 2]
    for level in plan.wide[:1] + plan.upper[::-1]:
        mine, rows, slot, _ = owned(level)
        count = plan.sources(level)

        @pl.when(mine)
        def _():
            wide_in[level][slot] = part[level - 1, rows]
            taken(wide_in[level].at[pl.ds(0, count - 1)], wide_r.at[level - 1]).wait()
            total = wide_in[level][0]
            for k in range(1, count):
                total = total + wide_in[level][k]
            final[level - 1, rows] = total

        gather(level, outer)
    for level in plan.narrow:
        rows = sep // 2**level
        total = part[level - 1, near_rows(level)]
        for m in range(1, 2**level):
            near_rs[level, m].wait_recv()
            total = total + near_in[level - 1, m - 1, pl.ds(0, rows)]
        final[level - 1, near_rows(level)] = total
        block = final.at[level - 1, near_rows(level)]
        for m in range(1, 2**level):
            near_ag[level, m] = sending(
                block, block, near_gs.at[level - 1, m - 1], near_gr.at[level - 1, m - 1], col_peer(2**level, m)
            )
    for level in plan.wide:
        gather(level, [c for c in range(n_col) if c not in outer])

    def applied(low, high):
        coef = final[low - 1 : high].reshape(sep * (high - low + 1), -1).astype(BF16)
        return jnp.dot(turned[:, sep * (low - 1) : sep * high], coef, preferred_element_type=F32)

    pair.wait_recv()
    final[0] = part[0] + l1_in[...]
    for copy in near_ag.values():
        copy.wait_recv()
    out_ref[...] += applied(1, low)

    even = half == 0
    passed = [
        remote(final.at[level - 1], passed_in.at[i], passed_s.at[i], passed_r.at[i], (row ^ 1, col))
        for i, level in enumerate(plan.upper)
    ]

    def arrived(level):
        mine = owned(level)[0]
        others = sep - plan.piece(level)

        @pl.when(mine)
        def _():
            taken(final.at[level - 1, pl.ds(0, others)], ag_r.at[level - 1]).wait()

        @pl.when(jnp.logical_not(mine))
        def _():
            taken(final.at[level - 1], ag_r.at[level - 1]).wait()

    @pl.when(even)
    def _():
        for level in reversed(plan.upper):
            arrived(level)
            passed[plan.upper.index(level)].start()

    arrived(plan.wide[0])

    @pl.when(even)
    def _():
        out_ref[...] += applied(low + 1, levels)
        for copy in passed:
            copy.wait_send()

    @pl.when(jnp.logical_not(even))
    def _():
        for copy in passed:
            copy.wait_recv()
        coef = jnp.concatenate([final[low], passed_in[...].reshape(len(plan.upper) * sep, -1)], axis=0)
        out_ref[...] += jnp.dot(turned[:, sep * low :], coef.astype(BF16), preferred_element_type=F32)

    sent += list(near_rs.values()) + list(near_ag.values())
    for copy in sent:
        copy.wait_send()
    for level in plan.wide:
        mine = owned(level)[0]
        mass = sep // plan.halves(level)
        rows = plan.piece(level)
        members = plan.row_span(level) * n_col

        @pl.when(mine)
        def _():
            taken(part.at[level - 1, pl.ds(0, mass - rows)], wide_s.at[level - 1]).wait()
            if plan.halves(level) == 1:
                taken(wide_in[level].at[pl.ds(0, members - 1)], ag_s.at[level - 1]).wait()

        @pl.when(jnp.logical_not(mine))
        def _():
            taken(part.at[level - 1, pl.ds(0, mass)], wide_s.at[level - 1]).wait()

        if plan.halves(level) == 2:

            @pl.when(jnp.logical_and(mine, even))
            def _():
                taken(wide_in[level].at[pl.ds(0, members // 2 - 1)], ag_s.at[level - 1]).wait()

            @pl.when(jnp.logical_and(mine, jnp.logical_not(even)))
            def _():
                taken(wide_in[level].at[pl.ds(0, members // 2)], ag_s.at[level - 1]).wait()


def in_one_kernel(plan, elem_residual, corners, share_rows, x_factor):
    rows_dev, cols = x_factor.shape
    shared = share_rows.shape[2]
    elems, kinds, width = elem_residual.shape
    levels, sep = plan.levels, plan.sep
    slots = max(1, plan.n_col // 2 - 1)
    dma = pltpu.SemaphoreType.DMA
    anywhere = pl.BlockSpec(memory_space=pl.ANY)
    return pl.pallas_call(
        functools.partial(kernel, plan),
        out_shape=pltpu.VMEM((rows_dev, width), F32),
        in_specs=[anywhere] * 4,
        out_specs=pl.BlockSpec(memory_space=pltpu.VMEM),
        scratch_shapes=[
            pltpu.VMEM((kinds, elems, width), BF16),
            pltpu.VMEM((kinds, elems), jnp.int32),
            pltpu.VMEM((2, shared), jnp.int32),
            pltpu.VMEM((cols, rows_dev), BF16),
            pltpu.VMEM((2, shared, width), F32),
            pltpu.VMEM((2, shared, width), F32),
            pltpu.VMEM((rows_dev, width), F32),
            pltpu.VMEM((rows_dev, width), BF16),
            pltpu.VMEM((levels, sep, width), F32),
            pltpu.VMEM((sep, width), F32),
            pltpu.VMEM((len(plan.upper), sep // 2, width), F32),
            pltpu.VMEM((levels, slots, sep // 4, width), F32),
            pltpu.VMEM((levels, sep, width), F32),
            pltpu.VMEM((rows_dev, sep * levels), BF16),
            pltpu.VMEM((len(plan.wide) * sep, 4 * shared), BF16),
            pltpu.VMEM((len(plan.upper), sep, width), F32),
            dma((kinds + 4,)),
            dma((2,)),
            dma((2,)),
            dma((1,)),
            dma((1,)),
            dma((len(plan.upper),)),
            dma((len(plan.upper),)),
            dma((1,)),
            dma((1,)),
            dma((levels, slots)),
            dma((levels, slots)),
            dma((levels, slots)),
            dma((levels, slots)),
            dma((levels,)),
            dma((levels,)),
            dma((levels,)),
            dma((levels,)),
        ]
        + [
            pltpu.VMEM((plan.row_span(level) * plan.n_col, plan.piece(level), width), F32)
            for level in plan.wide
        ],
        compiler_params=pltpu.CompilerParams(collective_id=0, has_side_effects=True),
        name="factor_solve",
    )(
        elem_residual.transpose(1, 0, 2),
        corners.T,
        share_rows.reshape(2, shared),
        x_factor.T,
    )


def solution(mesh):
    n_row, n_col = mesh.shape["row"], mesh.shape["col"]
    levels = (n_row * n_col).bit_length() - 1

    def per_device(elem_residual, corners, share_rows, x_factor):
        sep = (x_factor.shape[1] - INNER) // levels
        args = (elem_residual, corners, share_rows, x_factor)
        if takes(n_row, n_col, sep):
            return in_one_kernel(Plan(n_row, n_col, sep), *args)
        return by_rounds(n_row, n_col, *args)

    placed = (
        P(("row", "col"), None, None),
        P(("row", "col"), None),
        P(("row", "col"), None, None),
        P(("row", "col"), None),
    )
    return jax.shard_map(
        per_device, mesh=mesh, in_specs=placed, out_specs=P(("row", "col"), None), check_vma=False
    )
```

```python
import functools

import jax
import jax.numpy as jnp
from jax import lax
from jax.experimental import pallas as pl
from jax.experimental.pallas import tpu as pltpu
from jax.sharding import PartitionSpec as P

INNER = 1408
OUTER = (0, 2, 3, 1)
MESH = pl.DeviceIdType.MESH
F32 = jnp.float32
BF16 = jnp.bfloat16


def swapped(block, axis, stride):
    count = lax.axis_size(axis)
    route = []
    for low in range(count):
        high = low | 1 << stride
        if high != low and high < count:
            route += [(low, high), (high, low)]
    return lax.ppermute(block, axis, route)


def summed_levels(blocks, n_row, n_col):
    col_bits = n_col.bit_length() - 1
    row_bits = n_row.bit_length() - 1
    for bit in range(col_bits + row_bits):
        axis, stride = ("col", bit) if bit < col_bits else ("row", bit - col_bits)
        partner = swapped(blocks[bit:], axis, stride)
        blocks = jnp.concatenate([blocks[:bit], blocks[bit:] + partner], axis=0)
    return blocks


def by_rounds(n_row, n_col, elem_residual, corners, share_rows, x_factor):
    rows_dev = x_factor.shape[0]
    shared = share_rows.shape[2]
    width = elem_residual.shape[2]
    levels = (n_row * n_col).bit_length() - 1
    ext_len = rows_dev + 2 * shared
    flat_ids = corners.reshape(-1)
    onehot = (
        lax.broadcasted_iota(jnp.int32, (ext_len, flat_ids.shape[0]), 0) == flat_ids[None, :]
    ).astype(BF16)
    extended = jnp.dot(onehot, elem_residual.reshape(-1, width), preferred_element_type=F32)
    forward = [(i, (i + 1) % n_col) for i in range(n_col)]
    backward = [(target, source) for source, target in forward]
    from_left = lax.ppermute(extended[rows_dev + shared :], "col", forward)
    from_right = lax.ppermute(extended[rows_dev : rows_dev + shared], "col", backward)
    row_ids = lax.broadcasted_iota(jnp.int32, (rows_dev, shared), 0)
    assembled = extended[:rows_dev]
    for side, received in ((0, from_left), (1, from_right)):
        side_map = (row_ids == share_rows[0, side][None, :]).astype(F32)
        assembled = assembled + jnp.dot(
            side_map, received, precision=lax.Precision.HIGHEST, preferred_element_type=F32
        )
    partial_value = lax.dot_general(
        x_factor, assembled.astype(BF16), (((0,), (0,)), ((), ())), preferred_element_type=F32
    )
    blocks = partial_value[INNER:].reshape(levels, -1, width)
    blocks = summed_levels(blocks, n_row, n_col)
    coef = jnp.concatenate([partial_value[:INNER], blocks.reshape(-1, width)], axis=0)
    return jnp.dot(x_factor, coef.astype(BF16), preferred_element_type=F32)


class Plan:
    def __init__(self, n_row, n_col, sep):
        self.n_row, self.n_col, self.sep = n_row, n_col, sep
        self.levels = (n_row * n_col).bit_length() - 1
        self.col_bits = n_col.bit_length() - 1
        self.wide = list(range(self.col_bits, self.levels + 1))
        self.upper = self.wide[1:]
        self.narrow = list(range(self.col_bits - 1, 1, -1))

    def row_span(self, level):
        return max(1, 2**level // self.n_col)

    def halves(self, level):
        return 2 if self.row_span(level) > 1 else 1

    def piece(self, level):
        return self.sep // (self.n_col // 2 * self.halves(level))

    def sources(self, level):
        return self.row_span(level) // self.halves(level) * self.n_col

    def members(self, level):
        every = [(r, c) for r in range(self.row_span(level)) for c in range(self.n_col)]
        every = [at for at in every if at[0] % self.halves(level) == 0]
        return sorted(every, key=lambda at: (OUTER[at[1] * 4 // self.n_col], at[0] % 2, at[1], at[0]))


def takes(n_row, n_col, sep):
    return n_col >= 4 and 2 <= n_row <= 4 and sep % (8 * n_col) == 0


def tdot(a, b):
    return lax.dot_general(a, b, (((0,), (0,)), ((), ())), preferred_element_type=F32)


def kernel(
    plan,
    er_hbm, cor_hbm, sh_hbm, x_hbm,
    out_ref,
    er, cor, sh, xt,
    halo_out, halo_in, own, rhs, part, l1_in, pair_in, near_in, final, turned, shared_rows, passed_in,
    in_sem, halo_s, halo_r, pair_s, pair_r, passed_s, passed_r, l1_s, l1_r, near_s, near_r, near_gs, near_gr, wide_s, wide_r, ag_s, ag_r,
    *wide_in,
):
    row, col = lax.axis_index("row"), lax.axis_index("col")
    levels, n_row, n_col, sep = plan.levels, plan.n_row, plan.n_col, plan.sep
    rows_dev = out_ref.shape[0]
    shared = halo_out.shape[1]
    kinds = er.shape[0]
    elems = er.shape[1]
    wide_in = dict(zip(plan.wide, wide_in))

    right = (row, (col + 1) % n_col)
    left = (row, (col + n_col - 1) % n_col)
    first, last = n_col // 4, n_col // 4 * 3
    central = jnp.logical_and(col >= first, col < last)

    def col_peer(span, m):
        local = col % span
        return (row, col - local + (local + m) % span)

    def is_me(r, c):
        return jnp.logical_and(row == r, col == c)

    barrier = pltpu.get_barrier_semaphore()

    def greet(peer):
        pl.semaphore_signal(barrier, inc=1, device_id=peer, device_id_type=MESH)

    greet(left)
    greet(right)
    greet((row ^ 1, col))
    for level in plan.narrow:
        for m in range(1, 2**level):
            greet(col_peer(2**level, m))
    near = 3 + sum(2**level - 1 for level in plan.narrow)

    @pl.when(central)
    def _():
        for r in range(1, n_row):
            greet(((row + r) % n_row, col))
        for r in range(n_row):
            for c in range(1, n_col):
                greet(((row + r) % n_row, (col + c) % n_col))

    inner = xt.shape[0] - sep * levels
    low = plan.wide[0] - 1
    wide_at = inner + sep * low
    parts = [(cor_hbm, cor)]
    parts += [(er_hbm.at[k], er.at[k]) for k in range(kinds)]
    parts += [(sh_hbm, sh), (x_hbm.at[wide_at:], xt.at[wide_at:]), (x_hbm.at[:wide_at], xt.at[:wide_at])]
    loads = [
        pltpu.make_async_copy(source, target, in_sem.at[i]) for i, (source, target) in enumerate(parts)
    ]
    for load in loads[: kinds + 1]:
        load.start()

    def assembled_rows(start, count, start_done=True):
        total = None
        for k in range(kinds):
            if not start_done:
                loads[k + 1].wait()
            ids = cor[k : k + 1, :]
            at = lax.broadcasted_iota(jnp.int32, (count, elems), 0) + start
            onehot = jnp.where(at == ids, 1.0, 0.0).astype(BF16)
            term = jnp.dot(onehot, er[k], preferred_element_type=F32)
            total = term if total is None else total + term
        return total

    loads[0].wait()
    halo_out[...] = assembled_rows(rows_dev, 2 * shared, False).reshape(halo_out.shape)
    for load in loads[kinds + 1 :]:
        load.start()
    pl.semaphore_wait(barrier, near + n_row * n_col // 2 - central.astype(jnp.int32))

    def taken(buffer, sem):
        return pltpu.make_async_copy(buffer, buffer, sem)

    def remote(source, target, send, recv, peer):
        return pltpu.make_async_remote_copy(
            src_ref=source,
            dst_ref=target,
            send_sem=send,
            recv_sem=recv,
            device_id=peer,
            device_id_type=MESH,
        )

    def sending(*args):
        copy = remote(*args)
        copy.start()
        return copy

    sent = []
    away = col % 2
    near_side = 1 - away
    far_peer = (row, (col + n_col - 1 + 2 * away) % n_col)
    near_peer = (row, (col + n_col - 1 + 2 * near_side) % n_col)
    halo = [
        sending(halo_out.at[away], halo_in.at[near_side], halo_s.at[0], halo_r.at[near_side], far_peer),
        sending(halo_out.at[near_side], halo_in.at[away], halo_s.at[1], halo_r.at[away], near_peer),
    ]
    sent += halo

    def split(value):
        high = value.astype(BF16)
        return high, (value - high.astype(F32)).astype(BF16)

    own[...] = assembled_rows(0, rows_dev)
    loads[kinds + 1].wait()
    targets = jnp.concatenate([sh[0:1, :], sh[1:2, :]], axis=1)
    at = lax.broadcasted_iota(jnp.int32, (rows_dev, 2 * shared), 0)
    share_map = jnp.where(at == targets, 1.0, 0.0).astype(BF16)
    share_map = jnp.concatenate([share_map, share_map], axis=1)
    loads[kinds + 2].wait()
    rows = xt[wide_at:, :]
    high, fine = split(own[...])
    of_own = jnp.dot(rows, high, preferred_element_type=F32) + jnp.dot(rows, fine, preferred_element_type=F32)
    part[low:] = of_own.reshape(len(plan.wide), sep, -1)
    shared_rows[...] = jnp.dot(rows, share_map, preferred_element_type=F32).astype(BF16)
    loads[kinds + 3].wait()
    turned[...] = xt[inner:, :].T
    for side in range(2):
        taken(halo_in.at[side], halo_r.at[side]).wait()
    received = jnp.concatenate(split(halo_in[...].reshape(2 * shared, -1)), axis=0)
    block = jnp.dot(shared_rows[...], received, preferred_element_type=F32)
    part[low:] += block.reshape(len(plan.wide), sep, -1)

    half = row % 2

    def owned(level):
        span, halves = plan.row_span(level), plan.halves(level)
        base = row - row % span
        mine = jnp.logical_and(central, row == base + half * (span - 1))
        index = half * (halves - 1) * (n_col // 2) + (col - first)
        rows = plan.piece(level)
        slot = row % span // halves * n_col + col
        return mine, pl.ds(pl.multiple_of(jnp.where(mine, index, 0) * rows, 8), rows), slot, base

    def scatter(level):
        _, _, slot, base = owned(level)
        rows, halves = plan.piece(level), plan.halves(level)
        start = half * (halves - 1) * (sep // 2)
        target = base + half * (plan.row_span(level) - 1)
        for k in range(n_col // 2):
            c = jnp.where(col < n_col // 2, n_col // 2 - 1 - k, k)
            copy = remote(
                part.at[level - 1, pl.ds(pl.multiple_of(start + c * rows, 8), rows)],
                wide_in[level].at[slot],
                wide_s.at[level - 1],
                wide_r.at[level - 1],
                (target, first + c),
            )

            @pl.when(jnp.logical_not(is_me(target, first + c)))
            def _():
                copy.start()

    def gather(level, some):
        mine, rows, _, base = owned(level)
        block = final.at[level - 1, rows]

        @pl.when(mine)
        def _():
            for r, c in plan.members(level):
                if c in some:
                    copy = remote(block, block, ag_s.at[level - 1], ag_r.at[level - 1], (base + r, c))

                    @pl.when(jnp.logical_not(is_me(base + r, c)))
                    def _():
                        copy.start()

    kept = pl.ds(pl.multiple_of(half * (sep // 2), 8), sep // 2)
    given = pl.ds(pl.multiple_of((1 - half) * (sep // 2), 8), sep // 2)
    over = pl.ds(plan.upper[0] - 1, len(plan.upper))
    cores = sending(part.at[over, given], pair_in, pair_s.at[0], pair_r.at[0], (row ^ 1, col))
    sent.append(cores)
    scatter(plan.wide[0])
    assembled = own[...] + jnp.dot(share_map, received, preferred_element_type=F32)
    rhs[...] = assembled.astype(BF16)
    block = jnp.dot(xt[inner:wide_at, :], rhs[...], preferred_element_type=F32)
    part[:low] = block.reshape(low, sep, -1)

    def near_rows(level, ahead=0):
        span, rows = 2**level, sep // 2**level
        return pl.ds(pl.multiple_of((col % span + ahead) % span * rows, 8), rows)

    near_rs, near_ag = {}, {}
    for level in plan.narrow:
        for m in range(1, 2**level):
            near_rs[level, m] = sending(
                part.at[level - 1, near_rows(level, m)],
                near_in.at[level - 1, m - 1, pl.ds(0, sep // 2**level)],
                near_s.at[level - 1, m - 1],
                near_r.at[level - 1, m - 1],
                col_peer(2**level, m),
            )
    cores.wait_recv()
    for i, level in enumerate(plan.upper):
        part[level - 1, kept] += pair_in[i]
    for level in reversed(plan.upper):
        scatter(level)
    weights = jnp.dot(xt[:inner, :], rhs[...], preferred_element_type=F32).astype(BF16)
    out_ref[...] = tdot(xt[:inner, :], weights)

    pair = sending(part.at[0], l1_in, l1_s.at[0], l1_r.at[0], col_peer(2, 1))
    sent.append(pair)
    def gather_near():
        for level in plan.narrow:
            rows = sep // 2**level
            total = part[level - 1, near_rows(level)]
            for m in range(1, 2**level):
                near_rs[level, m].wait_recv()
                total = total + near_in[level - 1, m - 1, pl.ds(0, rows)]
            final[level - 1, near_rows(level)] = total
            block = final.at[level - 1, near_rows(level)]
            for m in range(1, 2**level):
                near_ag[level, m] = sending(
                    block, block, near_gs.at[level - 1, m - 1], near_gr.at[level - 1, m - 1], col_peer(2**level, m)
                )

    outer = [c for c in range(n_col) if OUTER[c * 4 // n_col] < 2]
    for level in plan.wide[:1] + plan.upper[::-1]:
        mine, rows, slot, _ = owned(level)
        count = plan.sources(level)

        @pl.when(mine)
        def _():
            wide_in[level][slot] = part[level - 1, rows]
            taken(wide_in[level].at[pl.ds(0, count - 1)], wide_r.at[level - 1]).wait()
            total = wide_in[level][0]
            for k in range(1, count):
                total = total + wide_in[level][k]
            final[level - 1, rows] = total

        gather(level, outer)
        if level == plan.wide[0]:
            gather_near()
    for level in plan.wide:
        gather(level, [c for c in range(n_col) if c not in outer])

    def applied(low, high):
        coef = final[low - 1 : high].reshape(sep * (high - low + 1), -1).astype(BF16)
        return jnp.dot(turned[:, sep * (low - 1) : sep * high], coef, preferred_element_type=F32)

    pair.wait_recv()
    final[0] = part[0] + l1_in[...]
    for copy in near_ag.values():
        copy.wait_recv()
    out_ref[...] += applied(1, low)

    even = half == 0
    passed = [
        remote(final.at[level - 1], passed_in.at[i], passed_s.at[i], passed_r.at[i], (row ^ 1, col))
        for i, level in enumerate(plan.upper)
    ]

    def arrived(level):
        mine = owned(level)[0]
        others = sep - plan.piece(level)

        @pl.when(mine)
        def _():
            taken(final.at[level - 1, pl.ds(0, others)], ag_r.at[level - 1]).wait()

        @pl.when(jnp.logical_not(mine))
        def _():
            taken(final.at[level - 1], ag_r.at[level - 1]).wait()

    @pl.when(even)
    def _():
        for level in reversed(plan.upper):
            arrived(level)
            passed[plan.upper.index(level)].start()

    arrived(plan.wide[0])

    @pl.when(even)
    def _():
        out_ref[...] += applied(low + 1, levels)
        for copy in passed:
            copy.wait_send()

    @pl.when(jnp.logical_not(even))
    def _():
        for copy in passed:
            copy.wait_recv()
        coef = jnp.concatenate([final[low], passed_in[...].reshape(len(plan.upper) * sep, -1)], axis=0)
        out_ref[...] += jnp.dot(turned[:, sep * low :], coef.astype(BF16), preferred_element_type=F32)

    sent += list(near_rs.values()) + list(near_ag.values())
    for copy in sent:
        copy.wait_send()
    for level in plan.wide:
        mine = owned(level)[0]
        mass = sep // plan.halves(level)
        rows = plan.piece(level)
        members = plan.row_span(level) * n_col

        @pl.when(mine)
        def _():
            taken(part.at[level - 1, pl.ds(0, mass - rows)], wide_s.at[level - 1]).wait()
            if plan.halves(level) == 1:
                taken(wide_in[level].at[pl.ds(0, members - 1)], ag_s.at[level - 1]).wait()

        @pl.when(jnp.logical_not(mine))
        def _():
            taken(part.at[level - 1, pl.ds(0, mass)], wide_s.at[level - 1]).wait()

        if plan.halves(level) == 2:

            @pl.when(jnp.logical_and(mine, even))
            def _():
                taken(wide_in[level].at[pl.ds(0, members // 2 - 1)], ag_s.at[level - 1]).wait()

            @pl.when(jnp.logical_and(mine, jnp.logical_not(even)))
            def _():
                taken(wide_in[level].at[pl.ds(0, members // 2)], ag_s.at[level - 1]).wait()


def in_one_kernel(plan, elem_residual, corners, share_rows, x_factor):
    rows_dev, cols = x_factor.shape
    shared = share_rows.shape[2]
    elems, kinds, width = elem_residual.shape
    levels, sep = plan.levels, plan.sep
    slots = max(1, plan.n_col // 2 - 1)
    dma = pltpu.SemaphoreType.DMA
    anywhere = pl.BlockSpec(memory_space=pl.ANY)
    return pl.pallas_call(
        functools.partial(kernel, plan),
        out_shape=pltpu.VMEM((rows_dev, width), F32),
        in_specs=[anywhere] * 4,
        out_specs=pl.BlockSpec(memory_space=pltpu.VMEM),
        scratch_shapes=[
            pltpu.VMEM((kinds, elems, width), BF16),
            pltpu.VMEM((kinds, elems), jnp.int32),
            pltpu.VMEM((2, shared), jnp.int32),
            pltpu.VMEM((cols, rows_dev), BF16),
            pltpu.VMEM((2, shared, width), F32),
            pltpu.VMEM((2, shared, width), F32),
            pltpu.VMEM((rows_dev, width), F32),
            pltpu.VMEM((rows_dev, width), BF16),
            pltpu.VMEM((levels, sep, width), F32),
            pltpu.VMEM((sep, width), F32),
            pltpu.VMEM((len(plan.upper), sep // 2, width), F32),
            pltpu.VMEM((levels, slots, sep // 4, width), F32),
            pltpu.VMEM((levels, sep, width), F32),
            pltpu.VMEM((rows_dev, sep * levels), BF16),
            pltpu.VMEM((len(plan.wide) * sep, 4 * shared), BF16),
            pltpu.VMEM((len(plan.upper), sep, width), F32),
            dma((kinds + 4,)),
            dma((2,)),
            dma((2,)),
            dma((1,)),
            dma((1,)),
            dma((len(plan.upper),)),
            dma((len(plan.upper),)),
            dma((1,)),
            dma((1,)),
            dma((levels, slots)),
            dma((levels, slots)),
            dma((levels, slots)),
            dma((levels, slots)),
            dma((levels,)),
            dma((levels,)),
            dma((levels,)),
            dma((levels,)),
        ]
        + [
            pltpu.VMEM((plan.row_span(level) * plan.n_col, plan.piece(level), width), F32)
            for level in plan.wide
        ],
        compiler_params=pltpu.CompilerParams(collective_id=0, has_side_effects=True),
        name="factor_solve",
    )(
        elem_residual.transpose(1, 0, 2),
        corners.T,
        share_rows.reshape(2, shared),
        x_factor.T,
    )


def solution(mesh):
    n_row, n_col = mesh.shape["row"], mesh.shape["col"]
    levels = (n_row * n_col).bit_length() - 1

    def per_device(elem_residual, corners, share_rows, x_factor):
        sep = (x_factor.shape[1] - INNER) // levels
        args = (elem_residual, corners, share_rows, x_factor)
        if takes(n_row, n_col, sep):
            return in_one_kernel(Plan(n_row, n_col, sep), *args)
        return by_rounds(n_row, n_col, *args)

    placed = (
        P(("row", "col"), None, None),
        P(("row", "col"), None),
        P(("row", "col"), None, None),
        P(("row", "col"), None),
    )
    return jax.shard_map(
        per_device, mesh=mesh, in_specs=placed, out_specs=P(("row", "col"), None), check_vma=False
    )
```

```python
import functools

import jax
import jax.numpy as jnp
from jax import lax
from jax.experimental import pallas as pl
from jax.experimental.pallas import tpu as pltpu
from jax.sharding import PartitionSpec as P

INNER = 1408
OUTER = (0, 2, 3, 1)
MESH = pl.DeviceIdType.MESH
F32 = jnp.float32
BF16 = jnp.bfloat16


def swapped(block, axis, stride):
    count = lax.axis_size(axis)
    route = []
    for low in range(count):
        high = low | 1 << stride
        if high != low and high < count:
            route += [(low, high), (high, low)]
    return lax.ppermute(block, axis, route)


def summed_levels(blocks, n_row, n_col):
    col_bits = n_col.bit_length() - 1
    row_bits = n_row.bit_length() - 1
    for bit in range(col_bits + row_bits):
        axis, stride = ("col", bit) if bit < col_bits else ("row", bit - col_bits)
        partner = swapped(blocks[bit:], axis, stride)
        blocks = jnp.concatenate([blocks[:bit], blocks[bit:] + partner], axis=0)
    return blocks


def by_rounds(n_row, n_col, elem_residual, corners, share_rows, x_factor):
    rows_dev = x_factor.shape[0]
    shared = share_rows.shape[2]
    width = elem_residual.shape[2]
    levels = (n_row * n_col).bit_length() - 1
    ext_len = rows_dev + 2 * shared
    flat_ids = corners.reshape(-1)
    onehot = (
        lax.broadcasted_iota(jnp.int32, (ext_len, flat_ids.shape[0]), 0) == flat_ids[None, :]
    ).astype(BF16)
    extended = jnp.dot(onehot, elem_residual.reshape(-1, width), preferred_element_type=F32)
    forward = [(i, (i + 1) % n_col) for i in range(n_col)]
    backward = [(target, source) for source, target in forward]
    from_left = lax.ppermute(extended[rows_dev + shared :], "col", forward)
    from_right = lax.ppermute(extended[rows_dev : rows_dev + shared], "col", backward)
    row_ids = lax.broadcasted_iota(jnp.int32, (rows_dev, shared), 0)
    assembled = extended[:rows_dev]
    for side, received in ((0, from_left), (1, from_right)):
        side_map = (row_ids == share_rows[0, side][None, :]).astype(F32)
        assembled = assembled + jnp.dot(
            side_map, received, precision=lax.Precision.HIGHEST, preferred_element_type=F32
        )
    partial_value = lax.dot_general(
        x_factor, assembled.astype(BF16), (((0,), (0,)), ((), ())), preferred_element_type=F32
    )
    blocks = partial_value[INNER:].reshape(levels, -1, width)
    blocks = summed_levels(blocks, n_row, n_col)
    coef = jnp.concatenate([partial_value[:INNER], blocks.reshape(-1, width)], axis=0)
    return jnp.dot(x_factor, coef.astype(BF16), preferred_element_type=F32)


class Plan:
    def __init__(self, n_row, n_col, sep):
        self.n_row, self.n_col, self.sep = n_row, n_col, sep
        self.levels = (n_row * n_col).bit_length() - 1
        self.col_bits = n_col.bit_length() - 1
        self.wide = list(range(self.col_bits, self.levels + 1))
        self.upper = self.wide[1:]
        self.narrow = list(range(self.col_bits - 1, 1, -1))

    def row_span(self, level):
        return max(1, 2**level // self.n_col)

    def halves(self, level):
        return 2 if self.row_span(level) > 1 else 1

    def piece(self, level):
        return self.sep // (self.n_col // 2 * self.halves(level))

    def sources(self, level):
        return self.row_span(level) // self.halves(level) * self.n_col

    def members(self, level):
        every = [(r, c) for r in range(self.row_span(level)) for c in range(self.n_col)]
        every = [at for at in every if at[0] % self.halves(level) == 0]
        return sorted(every, key=lambda at: (OUTER[at[1] * 4 // self.n_col], at[0] % 2, at[1], at[0]))


def takes(n_row, n_col, sep):
    return n_col >= 4 and 2 <= n_row <= 4 and sep % (8 * n_col) == 0


def tdot(a, b):
    return lax.dot_general(a, b, (((0,), (0,)), ((), ())), preferred_element_type=F32)


def kernel(
    plan,
    er_hbm, cor_hbm, sh_hbm, x_hbm,
    out_ref,
    er, cor, sh, xt,
    halo_out, halo_in, own, rhs, part, l1_in, pair_in, near_in, final, turned, shared_rows, passed_in,
    in_sem, halo_s, halo_r, pair_s, pair_r, passed_s, passed_r, l1_s, l1_r, near_s, near_r, near_gs, near_gr, wide_s, wide_r, ag_s, ag_r,
    *wide_in,
):
    row, col = lax.axis_index("row"), lax.axis_index("col")
    levels, n_row, n_col, sep = plan.levels, plan.n_row, plan.n_col, plan.sep
    rows_dev = out_ref.shape[0]
    shared = halo_out.shape[1]
    kinds = er.shape[0]
    elems = er.shape[1]
    wide_in = dict(zip(plan.wide, wide_in))

    right = (row, (col + 1) % n_col)
    left = (row, (col + n_col - 1) % n_col)
    first, last = n_col // 4, n_col // 4 * 3
    central = jnp.logical_and(col >= first, col < last)

    def col_peer(span, m):
        local = col % span
        return (row, col - local + (local + m) % span)

    def is_me(r, c):
        return jnp.logical_and(row == r, col == c)

    barrier = pltpu.get_barrier_semaphore()

    def greet(peer):
        pl.semaphore_signal(barrier, inc=1, device_id=peer, device_id_type=MESH)

    greet(left)
    greet(right)
    greet((row ^ 1, col))
    for level in plan.narrow:
        for m in range(1, 2**level):
            greet(col_peer(2**level, m))
    near = 3 + sum(2**level - 1 for level in plan.narrow)

    @pl.when(central)
    def _():
        for r in range(1, n_row):
            greet(((row + r) % n_row, col))
        for r in range(n_row):
            for c in range(1, n_col):
                greet(((row + r) % n_row, (col + c) % n_col))

    inner = xt.shape[0] - sep * levels
    low = plan.wide[0] - 1
    wide_at = inner + sep * low
    parts = [(cor_hbm, cor)]
    parts += [(er_hbm.at[k], er.at[k]) for k in range(kinds)]
    parts += [(sh_hbm, sh), (x_hbm.at[wide_at:], xt.at[wide_at:]), (x_hbm.at[:wide_at], xt.at[:wide_at])]
    loads = [
        pltpu.make_async_copy(source, target, in_sem.at[i]) for i, (source, target) in enumerate(parts)
    ]
    for load in loads[: kinds + 1]:
        load.start()

    def assembled_rows(start, count, start_done=True):
        total = None
        for k in range(kinds):
            if not start_done:
                loads[k + 1].wait()
            ids = cor[k : k + 1, :]
            at = lax.broadcasted_iota(jnp.int32, (count, elems), 0) + start
            onehot = jnp.where(at == ids, 1.0, 0.0).astype(BF16)
            term = jnp.dot(onehot, er[k], preferred_element_type=F32)
            total = term if total is None else total + term
        return total

    loads[0].wait()
    halo_out[...] = assembled_rows(rows_dev, 2 * shared, False).reshape(halo_out.shape)
    for load in loads[kinds + 1 :]:
        load.start()
    pl.semaphore_wait(barrier, near + n_row * n_col // 2 - central.astype(jnp.int32))

    def taken(buffer, sem):
        return pltpu.make_async_copy(buffer, buffer, sem)

    def remote(source, target, send, recv, peer):
        return pltpu.make_async_remote_copy(
            src_ref=source,
            dst_ref=target,
            send_sem=send,
            recv_sem=recv,
            device_id=peer,
            device_id_type=MESH,
        )

    def sending(*args):
        copy = remote(*args)
        copy.start()
        return copy

    sent = []
    away = col % 2
    near_side = 1 - away
    far_peer = (row, (col + n_col - 1 + 2 * away) % n_col)
    near_peer = (row, (col + n_col - 1 + 2 * near_side) % n_col)
    halo = [
        sending(halo_out.at[near_side], halo_in.at[away], halo_s.at[1], halo_r.at[away], near_peer),
        sending(halo_out.at[away], halo_in.at[near_side], halo_s.at[0], halo_r.at[near_side], far_peer),
    ]
    sent += halo

    def split(value):
        high = value.astype(BF16)
        return high, (value - high.astype(F32)).astype(BF16)

    own[...] = assembled_rows(0, rows_dev)
    loads[kinds + 1].wait()
    targets = jnp.concatenate([sh[0:1, :], sh[1:2, :]], axis=1)
    at = lax.broadcasted_iota(jnp.int32, (rows_dev, 2 * shared), 0)
    share_map = jnp.where(at == targets, 1.0, 0.0).astype(BF16)
    share_map = jnp.concatenate([share_map, share_map], axis=1)
    loads[kinds + 2].wait()
    rows = xt[wide_at:, :]
    high, fine = split(own[...])
    of_own = jnp.dot(rows, high, preferred_element_type=F32) + jnp.dot(rows, fine, preferred_element_type=F32)
    part[low:] = of_own.reshape(len(plan.wide), sep, -1)
    shared_rows[...] = jnp.dot(rows, share_map, preferred_element_type=F32).astype(BF16)
    loads[kinds + 3].wait()
    turned[...] = xt[inner:, :].T
    for side in range(2):
        taken(halo_in.at[side], halo_r.at[side]).wait()
    received = jnp.concatenate(split(halo_in[...].reshape(2 * shared, -1)), axis=0)
    block = jnp.dot(shared_rows[...], received, preferred_element_type=F32)
    part[low:] += block.reshape(len(plan.wide), sep, -1)

    half = row % 2

    def owned(level):
        span, halves = plan.row_span(level), plan.halves(level)
        base = row - row % span
        mine = jnp.logical_and(central, row == base + half * (span - 1))
        index = half * (halves - 1) * (n_col // 2) + (col - first)
        rows = plan.piece(level)
        slot = row % span // halves * n_col + col
        return mine, pl.ds(pl.multiple_of(jnp.where(mine, index, 0) * rows, 8), rows), slot, base

    def scatter(level):
        _, _, slot, base = owned(level)
        rows, halves = plan.piece(level), plan.halves(level)
        start = half * (halves - 1) * (sep // 2)
        target = base + half * (plan.row_span(level) - 1)
        for k in range(n_col // 2):
            c = jnp.where(col < n_col // 2, n_col // 2 - 1 - k, k)
            copy = remote(
                part.at[level - 1, pl.ds(pl.multiple_of(start + c * rows, 8), rows)],
                wide_in[level].at[slot],
                wide_s.at[level - 1],
                wide_r.at[level - 1],
                (target, first + c),
            )

            @pl.when(jnp.logical_not(is_me(target, first + c)))
            def _():
                copy.start()

    def gather(level, some):
        mine, rows, _, base = owned(level)
        block = final.at[level - 1, rows]

        @pl.when(mine)
        def _():
            for r, c in plan.members(level):
                if c in some:
                    copy = remote(block, block, ag_s.at[level - 1], ag_r.at[level - 1], (base + r, c))

                    @pl.when(jnp.logical_not(is_me(base + r, c)))
                    def _():
                        copy.start()

    kept = pl.ds(pl.multiple_of(half * (sep // 2), 8), sep // 2)
    given = pl.ds(pl.multiple_of((1 - half) * (sep // 2), 8), sep // 2)
    over = pl.ds(plan.upper[0] - 1, len(plan.upper))
    cores = sending(part.at[over, given], pair_in, pair_s.at[0], pair_r.at[0], (row ^ 1, col))
    sent.append(cores)
    scatter(plan.wide[0])
    assembled = own[...] + jnp.dot(share_map, received, preferred_element_type=F32)
    rhs[...] = assembled.astype(BF16)
    block = jnp.dot(xt[inner:wide_at, :], rhs[...], preferred_element_type=F32)
    part[:low] = block.reshape(low, sep, -1)

    def near_rows(level, ahead=0):
        span, rows = 2**level, sep // 2**level
        return pl.ds(pl.multiple_of((col % span + ahead) % span * rows, 8), rows)

    near_rs, near_ag = {}, {}
    for level in plan.narrow:
        for m in range(1, 2**level):
            near_rs[level, m] = sending(
                part.at[level - 1, near_rows(level, m)],
                near_in.at[level - 1, m - 1, pl.ds(0, sep // 2**level)],
                near_s.at[level - 1, m - 1],
                near_r.at[level - 1, m - 1],
                col_peer(2**level, m),
            )
    cores.wait_recv()
    for i, level in enumerate(plan.upper):
        part[level - 1, kept] += pair_in[i]
    for level in reversed(plan.upper):
        scatter(level)
    weights = jnp.dot(xt[:inner, :], rhs[...], preferred_element_type=F32).astype(BF16)
    out_ref[...] = tdot(xt[:inner, :], weights)

    pair = sending(part.at[0], l1_in, l1_s.at[0], l1_r.at[0], col_peer(2, 1))
    sent.append(pair)
    def gather_near():
        for level in plan.narrow:
            rows = sep // 2**level
            total = part[level - 1, near_rows(level)]
            for m in range(1, 2**level):
                near_rs[level, m].wait_recv()
                total = total + near_in[level - 1, m - 1, pl.ds(0, rows)]
            final[level - 1, near_rows(level)] = total
            block = final.at[level - 1, near_rows(level)]
            for m in range(1, 2**level):
                near_ag[level, m] = sending(
                    block, block, near_gs.at[level - 1, m - 1], near_gr.at[level - 1, m - 1], col_peer(2**level, m)
                )

    outer = [c for c in range(n_col) if OUTER[c * 4 // n_col] < 2]
    for level in plan.wide[:1] + plan.upper[::-1]:
        mine, rows, slot, _ = owned(level)
        count = plan.sources(level)

        @pl.when(mine)
        def _():
            wide_in[level][slot] = part[level - 1, rows]
            taken(wide_in[level].at[pl.ds(0, count - 1)], wide_r.at[level - 1]).wait()
            total = wide_in[level][0]
            for k in range(1, count):
                total = total + wide_in[level][k]
            final[level - 1, rows] = total

        gather(level, outer)
        if level == plan.wide[0]:
            gather_near()
    for level in plan.wide:
        gather(level, [c for c in range(n_col) if c not in outer])

    def applied(low, high):
        coef = final[low - 1 : high].reshape(sep * (high - low + 1), -1).astype(BF16)
        return jnp.dot(turned[:, sep * (low - 1) : sep * high], coef, preferred_element_type=F32)

    pair.wait_recv()
    final[0] = part[0] + l1_in[...]
    for copy in near_ag.values():
        copy.wait_recv()
    out_ref[...] += applied(1, low)

    even = half == 0
    passed = [
        remote(final.at[level - 1], passed_in.at[i], passed_s.at[i], passed_r.at[i], (row ^ 1, col))
        for i, level in enumerate(plan.upper)
    ]

    def arrived(level):
        mine = owned(level)[0]
        others = sep - plan.piece(level)

        @pl.when(mine)
        def _():
            taken(final.at[level - 1, pl.ds(0, others)], ag_r.at[level - 1]).wait()

        @pl.when(jnp.logical_not(mine))
        def _():
            taken(final.at[level - 1], ag_r.at[level - 1]).wait()

    @pl.when(even)
    def _():
        for level in reversed(plan.upper):
            arrived(level)
            passed[plan.upper.index(level)].start()

    arrived(plan.wide[0])

    @pl.when(even)
    def _():
        out_ref[...] += applied(low + 1, levels)
        for copy in passed:
            copy.wait_send()

    @pl.when(jnp.logical_not(even))
    def _():
        for copy in passed:
            copy.wait_recv()
        coef = jnp.concatenate([final[low], passed_in[...].reshape(len(plan.upper) * sep, -1)], axis=0)
        out_ref[...] += jnp.dot(turned[:, sep * low :], coef.astype(BF16), preferred_element_type=F32)

    sent += list(near_rs.values()) + list(near_ag.values())
    for copy in sent:
        copy.wait_send()
    for level in plan.wide:
        mine = owned(level)[0]
        mass = sep // plan.halves(level)
        rows = plan.piece(level)
        members = plan.row_span(level) * n_col

        @pl.when(mine)
        def _():
            taken(part.at[level - 1, pl.ds(0, mass - rows)], wide_s.at[level - 1]).wait()
            if plan.halves(level) == 1:
                taken(wide_in[level].at[pl.ds(0, members - 1)], ag_s.at[level - 1]).wait()

        @pl.when(jnp.logical_not(mine))
        def _():
            taken(part.at[level - 1, pl.ds(0, mass)], wide_s.at[level - 1]).wait()

        if plan.halves(level) == 2:

            @pl.when(jnp.logical_and(mine, even))
            def _():
                taken(wide_in[level].at[pl.ds(0, members // 2 - 1)], ag_s.at[level - 1]).wait()

            @pl.when(jnp.logical_and(mine, jnp.logical_not(even)))
            def _():
                taken(wide_in[level].at[pl.ds(0, members // 2)], ag_s.at[level - 1]).wait()


def in_one_kernel(plan, elem_residual, corners, share_rows, x_factor):
    rows_dev, cols = x_factor.shape
    shared = share_rows.shape[2]
    elems, kinds, width = elem_residual.shape
    levels, sep = plan.levels, plan.sep
    slots = max(1, plan.n_col // 2 - 1)
    dma = pltpu.SemaphoreType.DMA
    anywhere = pl.BlockSpec(memory_space=pl.ANY)
    return pl.pallas_call(
        functools.partial(kernel, plan),
        out_shape=pltpu.VMEM((rows_dev, width), F32),
        in_specs=[anywhere] * 4,
        out_specs=pl.BlockSpec(memory_space=pltpu.VMEM),
        scratch_shapes=[
            pltpu.VMEM((kinds, elems, width), BF16),
            pltpu.VMEM((kinds, elems), jnp.int32),
            pltpu.VMEM((2, shared), jnp.int32),
            pltpu.VMEM((cols, rows_dev), BF16),
            pltpu.VMEM((2, shared, width), F32),
            pltpu.VMEM((2, shared, width), F32),
            pltpu.VMEM((rows_dev, width), F32),
            pltpu.VMEM((rows_dev, width), BF16),
            pltpu.VMEM((levels, sep, width), F32),
            pltpu.VMEM((sep, width), F32),
            pltpu.VMEM((len(plan.upper), sep // 2, width), F32),
            pltpu.VMEM((levels, slots, sep // 4, width), F32),
            pltpu.VMEM((levels, sep, width), F32),
            pltpu.VMEM((rows_dev, sep * levels), BF16),
            pltpu.VMEM((len(plan.wide) * sep, 4 * shared), BF16),
            pltpu.VMEM((len(plan.upper), sep, width), F32),
            dma((kinds + 4,)),
            dma((2,)),
            dma((2,)),
            dma((1,)),
            dma((1,)),
            dma((len(plan.upper),)),
            dma((len(plan.upper),)),
            dma((1,)),
            dma((1,)),
            dma((levels, slots)),
            dma((levels, slots)),
            dma((levels, slots)),
            dma((levels, slots)),
            dma((levels,)),
            dma((levels,)),
            dma((levels,)),
            dma((levels,)),
        ]
        + [
            pltpu.VMEM((plan.row_span(level) * plan.n_col, plan.piece(level), width), F32)
            for level in plan.wide
        ],
        compiler_params=pltpu.CompilerParams(collective_id=0, has_side_effects=True),
        name="factor_solve",
    )(
        elem_residual.transpose(1, 0, 2),
        corners.T,
        share_rows.reshape(2, shared),
        x_factor.T,
    )


def solution(mesh):
    n_row, n_col = mesh.shape["row"], mesh.shape["col"]
    levels = (n_row * n_col).bit_length() - 1

    def per_device(elem_residual, corners, share_rows, x_factor):
        sep = (x_factor.shape[1] - INNER) // levels
        args = (elem_residual, corners, share_rows, x_factor)
        if takes(n_row, n_col, sep):
            return in_one_kernel(Plan(n_row, n_col, sep), *args)
        return by_rounds(n_row, n_col, *args)

    placed = (
        P(("row", "col"), None, None),
        P(("row", "col"), None),
        P(("row", "col"), None, None),
        P(("row", "col"), None),
    )
    return jax.shard_map(
        per_device, mesh=mesh, in_specs=placed, out_specs=P(("row", "col"), None), check_vma=False
    )
```

```python
import functools

import jax
import jax.numpy as jnp
from jax import lax
from jax.experimental import pallas as pl
from jax.experimental.pallas import tpu as pltpu
from jax.sharding import PartitionSpec as P

INNER = 1408
OUTER = (0, 2, 3, 1)
MESH = pl.DeviceIdType.MESH
F32 = jnp.float32
BF16 = jnp.bfloat16


def swapped(block, axis, stride):
    count = lax.axis_size(axis)
    route = []
    for low in range(count):
        high = low | 1 << stride
        if high != low and high < count:
            route += [(low, high), (high, low)]
    return lax.ppermute(block, axis, route)


def summed_levels(blocks, n_row, n_col):
    col_bits = n_col.bit_length() - 1
    row_bits = n_row.bit_length() - 1
    for bit in range(col_bits + row_bits):
        axis, stride = ("col", bit) if bit < col_bits else ("row", bit - col_bits)
        partner = swapped(blocks[bit:], axis, stride)
        blocks = jnp.concatenate([blocks[:bit], blocks[bit:] + partner], axis=0)
    return blocks


def by_rounds(n_row, n_col, elem_residual, corners, share_rows, x_factor):
    rows_dev = x_factor.shape[0]
    shared = share_rows.shape[2]
    width = elem_residual.shape[2]
    levels = (n_row * n_col).bit_length() - 1
    ext_len = rows_dev + 2 * shared
    flat_ids = corners.reshape(-1)
    onehot = (
        lax.broadcasted_iota(jnp.int32, (ext_len, flat_ids.shape[0]), 0) == flat_ids[None, :]
    ).astype(BF16)
    extended = jnp.dot(onehot, elem_residual.reshape(-1, width), preferred_element_type=F32)
    forward = [(i, (i + 1) % n_col) for i in range(n_col)]
    backward = [(target, source) for source, target in forward]
    from_left = lax.ppermute(extended[rows_dev + shared :], "col", forward)
    from_right = lax.ppermute(extended[rows_dev : rows_dev + shared], "col", backward)
    row_ids = lax.broadcasted_iota(jnp.int32, (rows_dev, shared), 0)
    assembled = extended[:rows_dev]
    for side, received in ((0, from_left), (1, from_right)):
        side_map = (row_ids == share_rows[0, side][None, :]).astype(F32)
        assembled = assembled + jnp.dot(
            side_map, received, precision=lax.Precision.HIGHEST, preferred_element_type=F32
        )
    partial_value = lax.dot_general(
        x_factor, assembled.astype(BF16), (((0,), (0,)), ((), ())), preferred_element_type=F32
    )
    blocks = partial_value[INNER:].reshape(levels, -1, width)
    blocks = summed_levels(blocks, n_row, n_col)
    coef = jnp.concatenate([partial_value[:INNER], blocks.reshape(-1, width)], axis=0)
    return jnp.dot(x_factor, coef.astype(BF16), preferred_element_type=F32)


class Plan:
    def __init__(self, n_row, n_col, sep):
        self.n_row, self.n_col, self.sep = n_row, n_col, sep
        self.levels = (n_row * n_col).bit_length() - 1
        self.col_bits = n_col.bit_length() - 1
        self.wide = list(range(self.col_bits, self.levels + 1))
        self.upper = self.wide[1:]
        self.narrow = list(range(self.col_bits - 1, 1, -1))

    def row_span(self, level):
        return max(1, 2**level // self.n_col)

    def halves(self, level):
        return 2 if self.row_span(level) > 1 else 1

    def piece(self, level):
        return self.sep // (self.n_col // 2 * self.halves(level))

    def sources(self, level):
        return self.row_span(level) // self.halves(level) * self.n_col

    def members(self, level):
        every = [(r, c) for r in range(self.row_span(level)) for c in range(self.n_col)]
        every = [at for at in every if at[0] % self.halves(level) == 0]
        return sorted(every, key=lambda at: (OUTER[at[1] * 4 // self.n_col], at[0] % 2, at[1], at[0]))


def takes(n_row, n_col, sep):
    return n_col >= 4 and 2 <= n_row <= 4 and sep % (8 * n_col) == 0


def tdot(a, b):
    return lax.dot_general(a, b, (((0,), (0,)), ((), ())), preferred_element_type=F32)


def kernel(
    plan,
    er_hbm, cor_hbm, sh_hbm, x_hbm,
    out_ref,
    er, cor, sh, xt,
    halo_out, halo_in, own, rhs, part, l1_in, pair_in, near_in, final, turned, shared_rows, passed_in,
    in_sem, halo_s, halo_r, pair_s, pair_r, passed_s, passed_r, l1_s, l1_r, near_s, near_r, near_gs, near_gr, wide_s, wide_r, ag_s, ag_r,
    *wide_in,
):
    row, col = lax.axis_index("row"), lax.axis_index("col")
    levels, n_row, n_col, sep = plan.levels, plan.n_row, plan.n_col, plan.sep
    rows_dev = out_ref.shape[0]
    shared = halo_out.shape[1]
    kinds = er.shape[0]
    elems = er.shape[1]
    wide_in = dict(zip(plan.wide, wide_in))

    right = (row, (col + 1) % n_col)
    left = (row, (col + n_col - 1) % n_col)
    first, last = n_col // 4, n_col // 4 * 3
    central = jnp.logical_and(col >= first, col < last)

    def col_peer(span, m):
        local = col % span
        return (row, col - local + (local + m) % span)

    def is_me(r, c):
        return jnp.logical_and(row == r, col == c)

    barrier = pltpu.get_barrier_semaphore()

    def greet(peer):
        pl.semaphore_signal(barrier, inc=1, device_id=peer, device_id_type=MESH)

    greet(left)
    greet(right)
    greet((row ^ 1, col))
    for level in plan.narrow:
        for m in range(1, 2**level):
            greet(col_peer(2**level, m))
    near = 3 + sum(2**level - 1 for level in plan.narrow)

    @pl.when(central)
    def _():
        for r in range(1, n_row):
            greet(((row + r) % n_row, col))
        for r in range(n_row):
            for c in range(1, n_col):
                greet(((row + r) % n_row, (col + c) % n_col))

    inner = xt.shape[0] - sep * levels
    low = plan.wide[0] - 1
    wide_at = inner + sep * low
    parts = [(cor_hbm, cor)]
    parts += [(er_hbm.at[k], er.at[k]) for k in range(kinds)]
    parts += [(sh_hbm, sh), (x_hbm.at[wide_at:], xt.at[wide_at:]), (x_hbm.at[:wide_at], xt.at[:wide_at])]
    loads = [
        pltpu.make_async_copy(source, target, in_sem.at[i]) for i, (source, target) in enumerate(parts)
    ]
    for load in loads[: kinds + 1]:
        load.start()

    def assembled_rows(start, count, start_done=True):
        total = None
        for k in range(kinds):
            if not start_done:
                loads[k + 1].wait()
            ids = cor[k : k + 1, :]
            at = lax.broadcasted_iota(jnp.int32, (count, elems), 0) + start
            onehot = jnp.where(at == ids, 1.0, 0.0).astype(BF16)
            term = jnp.dot(onehot, er[k], preferred_element_type=F32)
            total = term if total is None else total + term
        return total

    loads[0].wait()
    halo_out[...] = assembled_rows(rows_dev, 2 * shared, False).reshape(halo_out.shape)
    for load in loads[kinds + 1 :]:
        load.start()
    pl.semaphore_wait(barrier, near + n_row * n_col // 2 - central.astype(jnp.int32))

    def taken(buffer, sem):
        return pltpu.make_async_copy(buffer, buffer, sem)

    def remote(source, target, send, recv, peer):
        return pltpu.make_async_remote_copy(
            src_ref=source,
            dst_ref=target,
            send_sem=send,
            recv_sem=recv,
            device_id=peer,
            device_id_type=MESH,
        )

    def sending(*args):
        copy = remote(*args)
        copy.start()
        return copy

    sent = []
    away = col % 2
    near_side = 1 - away
    far_peer = (row, (col + n_col - 1 + 2 * away) % n_col)
    near_peer = (row, (col + n_col - 1 + 2 * near_side) % n_col)
    halo = [
        sending(halo_out.at[away], halo_in.at[near_side], halo_s.at[0], halo_r.at[near_side], far_peer),
        sending(halo_out.at[near_side], halo_in.at[away], halo_s.at[1], halo_r.at[away], near_peer),
    ]
    sent += halo

    def split(value):
        high = value.astype(BF16)
        return high, (value - high.astype(F32)).astype(BF16)

    own[...] = assembled_rows(0, rows_dev)
    loads[kinds + 1].wait()
    targets = jnp.concatenate([sh[0:1, :], sh[1:2, :]], axis=1)
    at = lax.broadcasted_iota(jnp.int32, (rows_dev, 2 * shared), 0)
    share_map = jnp.where(at == targets, 1.0, 0.0).astype(BF16)
    share_map = jnp.concatenate([share_map, share_map], axis=1)
    loads[kinds + 2].wait()
    rows = xt[wide_at:, :]
    high, fine = split(own[...])
    of_own = jnp.dot(rows, high, preferred_element_type=F32) + jnp.dot(rows, fine, preferred_element_type=F32)
    part[low:] = of_own.reshape(len(plan.wide), sep, -1)
    shared_rows[...] = jnp.dot(rows, share_map, preferred_element_type=F32).astype(BF16)
    loads[kinds + 3].wait()
    turned[...] = xt[inner:, :].T
    for side in range(2):
        taken(halo_in.at[side], halo_r.at[side]).wait()
    received = jnp.concatenate(split(halo_in[...].reshape(2 * shared, -1)), axis=0)
    block = jnp.dot(shared_rows[...], received, preferred_element_type=F32)
    part[low:] += block.reshape(len(plan.wide), sep, -1)

    half = row % 2

    def owned(level):
        span, halves = plan.row_span(level), plan.halves(level)
        base = row - row % span
        mine = jnp.logical_and(central, row == base + half * (span - 1))
        index = half * (halves - 1) * (n_col // 2) + (col - first)
        rows = plan.piece(level)
        slot = row % span // halves * n_col + col
        return mine, pl.ds(pl.multiple_of(jnp.where(mine, index, 0) * rows, 8), rows), slot, base

    def scatter(level):
        _, _, slot, base = owned(level)
        rows, halves = plan.piece(level), plan.halves(level)
        start = half * (halves - 1) * (sep // 2)
        target = base + half * (plan.row_span(level) - 1)
        for k in range(n_col // 2):
            c = jnp.where(col < n_col // 2, n_col // 2 - 1 - k, k)
            copy = remote(
                part.at[level - 1, pl.ds(pl.multiple_of(start + c * rows, 8), rows)],
                wide_in[level].at[slot],
                wide_s.at[level - 1],
                wide_r.at[level - 1],
                (target, first + c),
            )

            @pl.when(jnp.logical_not(is_me(target, first + c)))
            def _():
                copy.start()

    def gather(level, some):
        mine, rows, _, base = owned(level)
        block = final.at[level - 1, rows]

        @pl.when(mine)
        def _():
            for r, c in plan.members(level):
                if c in some:
                    copy = remote(block, block, ag_s.at[level - 1], ag_r.at[level - 1], (base + r, c))

                    @pl.when(jnp.logical_not(is_me(base + r, c)))
                    def _():
                        copy.start()

    kept = pl.ds(pl.multiple_of(half * (sep // 2), 8), sep // 2)
    given = pl.ds(pl.multiple_of((1 - half) * (sep // 2), 8), sep // 2)
    cores = {
        level: sending(
            part.at[level - 1, given], pair_in.at[i], pair_s.at[i], pair_r.at[i], (row ^ 1, col)
        )
        for i, level in reversed(list(enumerate(plan.upper)))
    }
    sent += list(cores.values())
    scatter(plan.wide[0])
    assembled = own[...] + jnp.dot(share_map, received, preferred_element_type=F32)
    rhs[...] = assembled.astype(BF16)
    block = jnp.dot(xt[inner:wide_at, :], rhs[...], preferred_element_type=F32)
    part[:low] = block.reshape(low, sep, -1)

    def near_rows(level, ahead=0):
        span, rows = 2**level, sep // 2**level
        return pl.ds(pl.multiple_of((col % span + ahead) % span * rows, 8), rows)

    near_rs, near_ag = {}, {}
    for level in plan.narrow:
        for m in range(1, 2**level):
            near_rs[level, m] = sending(
                part.at[level - 1, near_rows(level, m)],
                near_in.at[level - 1, m - 1, pl.ds(0, sep // 2**level)],
                near_s.at[level - 1, m - 1],
                near_r.at[level - 1, m - 1],
                col_peer(2**level, m),
            )
    for i, level in reversed(list(enumerate(plan.upper))):
        cores[level].wait_recv()
        part[level - 1, kept] += pair_in[i]
        scatter(level)
    weights = jnp.dot(xt[:inner, :], rhs[...], preferred_element_type=F32).astype(BF16)
    out_ref[...] = tdot(xt[:inner, :], weights)

    pair = sending(part.at[0], l1_in, l1_s.at[0], l1_r.at[0], col_peer(2, 1))
    sent.append(pair)
    def gather_near():
        for level in plan.narrow:
            rows = sep // 2**level
            total = part[level - 1, near_rows(level)]
            for m in range(1, 2**level):
                near_rs[level, m].wait_recv()
                total = total + near_in[level - 1, m - 1, pl.ds(0, rows)]
            final[level - 1, near_rows(level)] = total
            block = final.at[level - 1, near_rows(level)]
            for m in range(1, 2**level):
                near_ag[level, m] = sending(
                    block, block, near_gs.at[level - 1, m - 1], near_gr.at[level - 1, m - 1], col_peer(2**level, m)
                )

    outer = [c for c in range(n_col) if OUTER[c * 4 // n_col] < 2]
    for level in plan.wide[:1] + plan.upper[::-1]:
        mine, rows, slot, _ = owned(level)
        count = plan.sources(level)

        @pl.when(mine)
        def _():
            wide_in[level][slot] = part[level - 1, rows]
            taken(wide_in[level].at[pl.ds(0, count - 1)], wide_r.at[level - 1]).wait()
            total = wide_in[level][0]
            for k in range(1, count):
                total = total + wide_in[level][k]
            final[level - 1, rows] = total

        gather(level, outer)
        if level == plan.wide[0]:
            gather_near()
    for level in plan.wide:
        gather(level, [c for c in range(n_col) if c not in outer])

    def applied(low, high):
        coef = final[low - 1 : high].reshape(sep * (high - low + 1), -1).astype(BF16)
        return jnp.dot(turned[:, sep * (low - 1) : sep * high], coef, preferred_element_type=F32)

    pair.wait_recv()
    final[0] = part[0] + l1_in[...]
    for copy in near_ag.values():
        copy.wait_recv()
    out_ref[...] += applied(1, low)

    even = half == 0
    passed = [
        remote(final.at[level - 1], passed_in.at[i], passed_s.at[i], passed_r.at[i], (row ^ 1, col))
        for i, level in enumerate(plan.upper)
    ]

    def arrived(level):
        mine = owned(level)[0]
        others = sep - plan.piece(level)

        @pl.when(mine)
        def _():
            taken(final.at[level - 1, pl.ds(0, others)], ag_r.at[level - 1]).wait()

        @pl.when(jnp.logical_not(mine))
        def _():
            taken(final.at[level - 1], ag_r.at[level - 1]).wait()

    @pl.when(even)
    def _():
        for level in reversed(plan.upper):
            arrived(level)
            passed[plan.upper.index(level)].start()

    arrived(plan.wide[0])

    @pl.when(even)
    def _():
        out_ref[...] += applied(low + 1, levels)
        for copy in passed:
            copy.wait_send()

    @pl.when(jnp.logical_not(even))
    def _():
        for copy in passed:
            copy.wait_recv()
        coef = jnp.concatenate([final[low], passed_in[...].reshape(len(plan.upper) * sep, -1)], axis=0)
        out_ref[...] += jnp.dot(turned[:, sep * low :], coef.astype(BF16), preferred_element_type=F32)

    sent += list(near_rs.values()) + list(near_ag.values())
    for copy in sent:
        copy.wait_send()
    for level in plan.wide:
        mine = owned(level)[0]
        mass = sep // plan.halves(level)
        rows = plan.piece(level)
        members = plan.row_span(level) * n_col

        @pl.when(mine)
        def _():
            taken(part.at[level - 1, pl.ds(0, mass - rows)], wide_s.at[level - 1]).wait()
            if plan.halves(level) == 1:
                taken(wide_in[level].at[pl.ds(0, members - 1)], ag_s.at[level - 1]).wait()

        @pl.when(jnp.logical_not(mine))
        def _():
            taken(part.at[level - 1, pl.ds(0, mass)], wide_s.at[level - 1]).wait()

        if plan.halves(level) == 2:

            @pl.when(jnp.logical_and(mine, even))
            def _():
                taken(wide_in[level].at[pl.ds(0, members // 2 - 1)], ag_s.at[level - 1]).wait()

            @pl.when(jnp.logical_and(mine, jnp.logical_not(even)))
            def _():
                taken(wide_in[level].at[pl.ds(0, members // 2)], ag_s.at[level - 1]).wait()


def in_one_kernel(plan, elem_residual, corners, share_rows, x_factor):
    rows_dev, cols = x_factor.shape
    shared = share_rows.shape[2]
    elems, kinds, width = elem_residual.shape
    levels, sep = plan.levels, plan.sep
    slots = max(1, plan.n_col // 2 - 1)
    dma = pltpu.SemaphoreType.DMA
    anywhere = pl.BlockSpec(memory_space=pl.ANY)
    return pl.pallas_call(
        functools.partial(kernel, plan),
        out_shape=pltpu.VMEM((rows_dev, width), F32),
        in_specs=[anywhere] * 4,
        out_specs=pl.BlockSpec(memory_space=pltpu.VMEM),
        scratch_shapes=[
            pltpu.VMEM((kinds, elems, width), BF16),
            pltpu.VMEM((kinds, elems), jnp.int32),
            pltpu.VMEM((2, shared), jnp.int32),
            pltpu.VMEM((cols, rows_dev), BF16),
            pltpu.VMEM((2, shared, width), F32),
            pltpu.VMEM((2, shared, width), F32),
            pltpu.VMEM((rows_dev, width), F32),
            pltpu.VMEM((rows_dev, width), BF16),
            pltpu.VMEM((levels, sep, width), F32),
            pltpu.VMEM((sep, width), F32),
            pltpu.VMEM((len(plan.upper), sep // 2, width), F32),
            pltpu.VMEM((levels, slots, sep // 4, width), F32),
            pltpu.VMEM((levels, sep, width), F32),
            pltpu.VMEM((rows_dev, sep * levels), BF16),
            pltpu.VMEM((len(plan.wide) * sep, 4 * shared), BF16),
            pltpu.VMEM((len(plan.upper), sep, width), F32),
            dma((kinds + 4,)),
            dma((2,)),
            dma((2,)),
            dma((len(plan.upper),)),
            dma((len(plan.upper),)),
            dma((len(plan.upper),)),
            dma((len(plan.upper),)),
            dma((1,)),
            dma((1,)),
            dma((levels, slots)),
            dma((levels, slots)),
            dma((levels, slots)),
            dma((levels, slots)),
            dma((levels,)),
            dma((levels,)),
            dma((levels,)),
            dma((levels,)),
        ]
        + [
            pltpu.VMEM((plan.row_span(level) * plan.n_col, plan.piece(level), width), F32)
            for level in plan.wide
        ],
        compiler_params=pltpu.CompilerParams(collective_id=0, has_side_effects=True),
        name="factor_solve",
    )(
        elem_residual.transpose(1, 0, 2),
        corners.T,
        share_rows.reshape(2, shared),
        x_factor.T,
    )


def solution(mesh):
    n_row, n_col = mesh.shape["row"], mesh.shape["col"]
    levels = (n_row * n_col).bit_length() - 1

    def per_device(elem_residual, corners, share_rows, x_factor):
        sep = (x_factor.shape[1] - INNER) // levels
        args = (elem_residual, corners, share_rows, x_factor)
        if takes(n_row, n_col, sep):
            return in_one_kernel(Plan(n_row, n_col, sep), *args)
        return by_rounds(n_row, n_col, *args)

    placed = (
        P(("row", "col"), None, None),
        P(("row", "col"), None),
        P(("row", "col"), None, None),
        P(("row", "col"), None),
    )
    return jax.shard_map(
        per_device, mesh=mesh, in_specs=placed, out_specs=P(("row", "col"), None), check_vma=False
    )
```
